32 devices in a mesh: seq: 16 (over z, y, core), pair: 2 (over x).
Axes of the slice: x: 2, y: 2, z: 4, core: 2. Of those that a mesh axis runs over, the one named last changes fastest.
Arguments:
- inputs: bfloat16 [8192, 1024], P('seq'), may hold values from -6 to 6
- cotangent: bfloat16 [8192, 1024], P('seq'), may hold values from -6 to 6
- doc_lengths: int32 [1, 8], replicated, may hold values from 1 to 4096, 8192 in all within a row
- pad_counts: int32 [1], replicated, may hold values from 0 to 2047
- ln_gain: float32 [1024], replicated, may hold values from 0.5 to 1.5
- ln_bias: float32 [1024], replicated, may hold values from -4 to 4
- w_first: bfloat16 [2, 1024, 4096], P('pair'), may hold values from -1.5 to 1.5
- b_first: float32 [2, 4096], P('pair'), may hold values from -4 to 4
- w_second: bfloat16 [4096, 1024], replicated, may hold values from -0.09375 to 0.09375
- b_second: float32 [1024], replicated, may hold values from -4 to 4
Outputs:
- outputs: bfloat16 [8192, 1024], P('seq')
- d_inputs: bfloat16 [8192, 1024], P('seq')
- d_gain: float32 [1024], replicated
- d_bias: float32 [1024], replicated
- d_w_first: float32 [2, 1024, 4096], P('pair')
- d_b_first: float32 [2, 4096], P('pair')
- d_w_second: float32 [4096, 1024], P('pair')
- d_b_second: float32 [1024], replicated
The draws below stay inside these ranges and needn't reach their ends.
Inputs may be any that keep to these rules, and one draw needn't show every extreme that they name: `doc_lengths`: each row holds 8 document lengths that sum to 8192; the longest is exactly 4096.
All inputs are finite; a program needn't handle non-finite values.
Results may differ from the reference program's by a relative error of at most 0.0065.
Values may be sent and summed in bfloat16 or wider, within the bound.
No kernel may reach another device: no remote copies, remote signals or barrier semaphores. Data moves between devices by JAX's collectives and lax.ppermute only.
A program may use at most 576 MiB of HBM per device.

```python
import math
import jax
import jax.numpy as jnp
import numpy as np
from jax import lax

HEADS = 16
HEAD_DIM = 64
D = 1024
FF = 4096
ROT = 16
SEQ_LEN = 8192
DOCS = 8
MOST_DOC = 4096
PAD_MAX = 2048
LEAD_ROWS = 4096
TOKENS = 8192
NSEQ = 1


out_scale = 0.25


def draw_w_first(key, part):
    values = jnp.clip(jax.random.normal(key, (2, D, FF), jnp.float32), -6.0, 6.0)
    column = jnp.arange(FF)[None, None, :]
    slot_index = jnp.arange(2)[:, None, None]
    factor = jnp.where((slot_index == 0) & (column >= 3 * D), out_scale, D ** (-0.5))
    return (values * factor).astype(jnp.bfloat16)


def level_of(key, shape, cuts, smallest, largest):
    level, own = 1.0, jax.random.fold_in(key, 6)
    for dim, parts in cuts:
        draws = jnp.exp(jax.random.uniform(jax.random.fold_in(own, dim), (parts,), jnp.float32, smallest / len(cuts), largest / len(cuts)))
        level = level * jnp.repeat(draws, shape[dim] // parts).reshape([-1 if axis == dim else 1 for axis in range(len(shape))])
    return level


def split_up(count, total, bound, slope):
    weights = [(1 << 20) // math.isqrt(standing ** slope) + 1 for standing in range(2, count + 1)]
    spare, holding = total - bound - (count - 1), [1] * (count - 1)
    while spare > 0:
        candidates = [i for i in range(count - 1) if holding[i] < bound]
        mass, remaining = sum([weights[i] for i in candidates]), spare
        for i in candidates:
            addition = min(bound - holding[i], max(1, remaining * weights[i] // mass), spare)
            holding[i] = holding[i] + addition
            spare = spare - addition
    return np.array([bound] + holding)


def uneven_parts(rng, count, total, bound, slope):
    if count == 2:
        one = jax.random.randint(rng, (), max(1, total - bound), min(bound, total - 1) + 1)
        return jnp.stack([one, total - one])
    sizes = jnp.asarray(split_up(count, total, bound, slope), jnp.int32)
    twos = (count - 1) // 2
    donor, taker = sizes[1:1 + 2 * twos:2], sizes[2:2 + 2 * twos:2]
    room = jnp.minimum(donor - 1, bound - taker)
    passed = jax.random.randint(jax.random.fold_in(rng, 1), (twos,), 0, 1 << 20) % (room + 1)
    sizes = sizes.at[1:1 + 2 * twos:2].set(donor - passed).at[2:2 + 2 * twos:2].set(taker + passed)
    return sizes[jax.random.permutation(jax.random.fold_in(rng, 2), count)]


def scatter_about(rng, extent, spread, bound, cuts=(), kind=jnp.bfloat16):
    factor_of = level_of(rng, extent, cuts, -0.22, 0.18) if cuts else 1.0
    drawn = jax.random.normal(rng, extent, jnp.float32) * spread * factor_of
    return jnp.minimum(jnp.maximum(drawn, -bound), bound).astype(kind)


def setup_inputs(seed: int = 0) -> dict:
    keys = jax.random.split(jax.random.key(seed), 11)
    inputs = scatter_about(keys[0], (TOKENS, D), 1.0, 6.0, ((0, 16),))
    cotangent = scatter_about(keys[1], (TOKENS, D), 1.0, 6.0, ((0, 16),))
    doc_lengths = jax.vmap(lambda own: uneven_parts(own, DOCS, SEQ_LEN, MOST_DOC, 2))(jax.random.split(keys[2], NSEQ)).reshape((NSEQ, DOCS)).astype(jnp.int32)
    pad_counts = jax.random.randint(keys[3], (NSEQ,), 0, PAD_MAX).astype(jnp.int32)
    ln_gain = jnp.clip(1.0 + 0.1 * jax.random.normal(keys[4], (D,), jnp.float32), 0.5, 1.5)
    ln_bias = scatter_about(keys[5], (D,), 0.3, 4.0, (), jnp.float32)
    w_first = draw_w_first(jax.random.fold_in(keys[10], 71), 0)
    b_first = scatter_about(keys[7], (2, FF), 0.3, 4.0, ((0, 2),), jnp.float32)
    w_second = scatter_about(keys[8], (FF, D), FF ** -0.5, 0.09375)
    b_second = scatter_about(keys[9], (D,), 0.3, 4.0, (), jnp.float32)
    return {"inputs": inputs, "cotangent": cotangent, "doc_lengths": doc_lengths, "pad_counts": pad_counts, "ln_gain": ln_gain, "ln_bias": ln_bias, "w_first": w_first, "b_first": b_first, "w_second": w_second, "b_second": b_second}


@jax.custom_vjp
def low(v):
    return lax.optimization_barrier(v.astype(jnp.bfloat16)).astype(jnp.float32)

@jax.custom_vjp
def low_back(v):
    return v

def low_keep(v):
    return (low(v), None)

def low_pass(kept, grad):
    return (grad,)

def back_keep(v):
    return (v, None)

def back_low(kept, grad):
    return (low(grad),)
low.defvjp(low_keep, low_pass)
low_back.defvjp(back_keep, back_low)
epsilon = 1e-05
masked_fill = -1e+30

def matmul(left, right):
    return jnp.dot(left, right, precision=lax.Precision.HIGHEST, preferred_element_type=jnp.float32)

def normalize(tok_block, ln_gain, ln_bias):
    centred = tok_block - lax.optimization_barrier(jnp.mean(tok_block, axis=1, keepdims=True))
    variance = lax.optimization_barrier(jnp.mean(centred * centred, axis=1, keepdims=True))
    return centred * lax.rsqrt(variance + epsilon) * ln_gain + ln_bias

def angles_for(offsets):
    freq_index = jnp.arange(ROT // 2, dtype=jnp.float32)
    inverse = 10000.0 ** (-2.0 * freq_index / ROT)
    angle_tab = offsets.astype(jnp.float32)[:, None] * inverse[None, :]
    return (jnp.cos(angle_tab)[:, None, :], jnp.sin(angle_tab)[:, None, :])

def rotate(tensor, cos_tab, sine_tab):
    lower_part = tensor[..., :ROT // 2]
    upper_part = tensor[..., ROT // 2:ROT]
    return jnp.concatenate([lower_part * cos_tab - upper_part * sine_tab, upper_part * cos_tab + lower_part * sine_tab, tensor[..., ROT:]], axis=-1)

def attend_sequence(members):
    queries, keys_rot, values, segment, padding = members
    places = jnp.arange(SEQ_LEN, dtype=jnp.int32)
    allowed = (segment[:, None] == segment[None, :]) & (places[None, :] <= places[:, None]) & (jnp.logical_not(padding)[None, :] | (places[None, :] == places[:, None]))

    def one_head(head_parts):
        head_query, head_keys, head_values = head_parts
        scores = low_back(matmul(head_query, head_keys.T) * HEAD_DIM ** (-0.5))
        masked = jnp.where(allowed, scores, masked_fill)
        exponent = jnp.exp(masked - lax.optimization_barrier(jnp.max(masked, axis=1, keepdims=True)))
        probabilities = exponent / lax.optimization_barrier(jnp.sum(exponent, axis=1, keepdims=True))
        return matmul(low(probabilities), head_values)
    results = lax.map(jax.checkpoint(one_head), (jnp.transpose(queries, (1, 0, 2)), jnp.transpose(keys_rot, (1, 0, 2)), jnp.transpose(values, (1, 0, 2))))
    return jnp.transpose(results, (1, 0, 2))

def reference(inputs, cotangent, doc_lengths, pad_counts, ln_gain, ln_bias, w_first, b_first, w_second, b_second):
    first_wide = w_first.astype(jnp.float32)
    second_wide = w_second.astype(jnp.float32)
    positions = jnp.arange(TOKENS, dtype=jnp.int32)
    bounds = jnp.cumsum(doc_lengths, axis=1)
    seq_of = positions // SEQ_LEN
    offsets = positions % SEQ_LEN
    doc_ids = lax.optimization_barrier(jnp.sum((offsets[:, None] >= bounds[seq_of]).astype(jnp.int32), axis=1))
    padding = offsets >= SEQ_LEN - pad_counts[seq_of]
    segment = jnp.where(padding, DOCS, doc_ids)
    cos_tab, sine_tab = angles_for(offsets)

    def forward(tok_block, gain_in, bias_in, w_qkv, b_qkv, w_out, b_out, w_up, b_up, w_down, b_down):
        hidden = low(normalize(tok_block, gain_in, bias_in))
        projected = low_back(matmul(hidden, w_qkv) + b_qkv)
        per_head = projected.reshape(TOKENS, 3, HEADS, HEAD_DIM)
        queries = low(rotate(per_head[:, 0], cos_tab, sine_tab))
        keys_rot = low(rotate(per_head[:, 1], cos_tab, sine_tab))
        values = low(per_head[:, 2])
        shape_seq = (NSEQ, SEQ_LEN, HEADS, HEAD_DIM)
        attended = lax.map(jax.checkpoint(attend_sequence), (queries.reshape(shape_seq), keys_rot.reshape(shape_seq), values.reshape(shape_seq), segment.reshape(NSEQ, SEQ_LEN), padding.reshape(NSEQ, SEQ_LEN)))
        attended = low_back(low(attended.reshape(TOKENS, D)))
        attention_out = matmul(attended, w_out) + b_out
        up_proj = low_back(matmul(hidden, w_up) + b_up)
        active = low(jax.nn.gelu(up_proj, approximate=False))
        feed_out = matmul(active, w_down) + b_down
        return tok_block + attention_out + feed_out
    widened = jnp.roll(inputs.astype(jnp.float32), -LEAD_ROWS, axis=0)
    result, backward = jax.vjp(forward, widened, ln_gain, ln_bias, first_wide[0, :, :3 * D], b_first[0, :3 * D], first_wide[0, :, 3 * D:], b_first[0, 3 * D:], first_wide[1], b_first[1], second_wide, b_second)
    gradients = backward(jnp.roll(cotangent.astype(jnp.float32), -LEAD_ROWS, axis=0))
    d_tokens, d_gain, d_bias, d_qkv, d_qkv_bias, d_out, d_out_bias, d_up, d_up_bias, d_down, d_down_bias = gradients
    d_w_first = jnp.stack([jnp.concatenate([d_qkv, d_out], axis=1), d_up])
    d_b_first = jnp.stack([jnp.concatenate([d_qkv_bias, d_out_bias]), d_up_bias])
    result = jnp.roll(result, LEAD_ROWS, axis=0)
    d_tokens = jnp.roll(d_tokens, LEAD_ROWS, axis=0)
    return (result.astype(jnp.bfloat16), d_tokens.astype(jnp.bfloat16), d_gain, d_bias, d_w_first, d_b_first, d_down, d_down_bias)
```

```python
import functools

import jax
import jax.numpy as jnp
from jax import lax
from jax.experimental import pallas as pl
from jax.experimental.pallas import tpu as pltpu
from jax.sharding import PartitionSpec as P

HEADS = 16
HEAD_DIM = 64
D = 1024
FF = 4096
ROT = 16
SEQ_LEN = 8192
DOCS = 8

BQ = 256
BK = 512
epsilon = 1e-05
masked_fill = -1e30
bf16 = jnp.bfloat16
f32 = jnp.float32
VMEM_LIMIT = 60 * 1024 * 1024


def mm(left, right, dims):
    return lax.dot_general(left, right, (dims, ((), ())), preferred_element_type=f32)


def rotation_tables(positions, period):
    lane = lax.broadcasted_iota(jnp.int32, (positions.shape[0], 128), 1) % period
    inverse = 10000.0 ** (-2.0 * (lane % (ROT // 2)).astype(f32) / ROT)
    angle = positions.astype(f32)[:, None] * inverse
    cos_tab = jnp.where(lane < ROT, jnp.cos(angle), 1.0)
    sine = jnp.sin(angle)
    sine_tab = jnp.where(lane < ROT // 2, -sine, jnp.where(lane < ROT, sine, 0.0))
    return cos_tab, sine_tab


def turn(block, cos_tab, sine_tab, lane):
    from_left = pltpu.roll(block, 8, 1)
    from_right = pltpu.roll(block, 120, 1)
    return block * cos_tab + jnp.where(lane % 64 < 8, from_right, from_left) * sine_tab


def project_kernel(h_ref, g_ref, wq, wk, wv, wo, bq, bk, bv, c_ref, s_ref, out):
    rows = h_ref.shape[0]
    lane = lax.broadcasted_iota(jnp.int32, (rows, 128), 1)
    low = lane < 64
    hidden = h_ref[...]
    q_all = mm(hidden, wq[...], ((1,), (0,))) + bq[...]
    k_all = mm(hidden, wk[...], ((1,), (0,))) + bk[...]
    v_all = mm(hidden, wv[...], ((1,), (0,))) + bv[...]
    g_all = mm(g_ref[...], wo[...], ((1,), (1,)))
    cos_tab = c_ref[...]
    sine_tab = s_ref[...]
    for pair in range(2):
        cut = slice(128 * pair, 128 * pair + 128)
        q = turn(q_all[:, cut], cos_tab, sine_tab, lane)
        k = turn(k_all[:, cut], cos_tab, sine_tab, lane)
        v = v_all[:, cut]
        g = g_all[:, cut]
        out[2 * pair, 0] = jnp.where(low, q, pltpu.roll(g, 64, 1)).astype(bf16)
        out[2 * pair, 1] = jnp.where(low, k, pltpu.roll(v, 64, 1)).astype(bf16)
        out[2 * pair + 1, 0] = jnp.where(low, pltpu.roll(q, 64, 1), g).astype(bf16)
        out[2 * pair + 1, 1] = jnp.where(low, pltpu.roll(k, 64, 1), v).astype(bf16)


def project(hidden, cotangent, weights, biases, cos_tab, sine_tab):
    rows = hidden.shape[0]
    whole = lambda i: (0, 0)
    steps = HEADS // 4
    return pl.pallas_call(
        project_kernel,
        grid=(steps,),
        in_specs=[
            pl.BlockSpec((rows, D), whole),
            pl.BlockSpec((rows, D), whole),
            pl.BlockSpec((D, 256), lambda i: (0, i)),
            pl.BlockSpec((D, 256), lambda i: (0, i + steps)),
            pl.BlockSpec((D, 256), lambda i: (0, i + 2 * steps)),
            pl.BlockSpec((256, D), lambda i: (i, 3)),
            pl.BlockSpec((1, 256), lambda i: (0, i)),
            pl.BlockSpec((1, 256), lambda i: (0, i + steps)),
            pl.BlockSpec((1, 256), lambda i: (0, i + 2 * steps)),
            pl.BlockSpec((rows, 128), whole),
            pl.BlockSpec((rows, 128), whole),
        ],
        out_specs=pl.BlockSpec((4, 2, rows, 128), lambda i: (i, 0, 0, 0)),
        out_shape=jax.ShapeDtypeStruct((HEADS, 2, rows, 128), bf16),
        compiler_params=pltpu.CompilerParams(vmem_limit_bytes=VMEM_LIMIT),
        name="project",
    )(hidden, cotangent, weights, weights, weights, weights, biases, biases, biases,
      cos_tab, sine_tab)


def attend_kernel(scal, lo_ref, x_ref, kvp_ref, dq_ref, own_ref, send_ref,
                  kv_s, kvt_s, s_buf, p_buf, acc_s):
    members, _, rows, _ = x_ref.shape
    place = scal[0]
    parity = scal[1]
    scale = HEAD_DIM ** (-0.5)
    to_two = scale * 1.4426950408889634

    for m in range(members):
        d = (place - m + members) % members
        at_own = pl.multiple_of((2 * m + parity) * rows, rows)
        at_other = pl.multiple_of((2 * m + 1 - parity) * rows, rows)
        kv_s[pl.ds(at_own, rows), :] = x_ref[d, 1]
        kv_s[pl.ds(at_other, rows), :] = kvp_ref[d]
    acc_s[...] = jnp.zeros_like(acc_s)

    def transpose_step(b, carry):
        at = pl.multiple_of(b * 256, 256)
        kvt_s[:, pl.ds(at, 256)] = kv_s[pl.ds(at, 256), :].astype(f32).T.astype(bf16)
        return carry

    lax.fori_loop(0, kv_s.shape[0] // 256, transpose_step, 0)

    per = rows // BQ
    lane = lax.broadcasted_iota(jnp.int32, (BQ, 128), 1)
    key_iota = lax.broadcasted_iota(jnp.int32, (BK, BQ), 0)
    query_iota = lax.broadcasted_iota(jnp.int32, (1, BQ), 1)

    def query_block(i, carry):
        m = i // per
        part = i % per
        d = (place - m + members) % members
        off = pl.multiple_of(part * BQ, BQ)
        first = (2 * m + parity) * rows + off
        qd = x_ref[d, 0, pl.ds(off, BQ), :]
        zero = jnp.zeros_like(qd)
        qz = jnp.where(lane < 64, qd, zero)
        dz = jnp.where(lane < 64, zero, qd)
        both = jnp.concatenate([qz, dz], axis=0)
        kb0 = scal[2 + i] // BK
        kb1 = (first + BQ - 1) // BK + 1
        qpos = first + query_iota
        lo = lo_ref[pl.ds(i, 1), :]

        def scores_step(kb, mx):
            at = pl.multiple_of(kb * BK, BK)
            r = mm(kv_s[pl.ds(at, BK), :], both, ((1,), (1,)))
            kpos = at + key_iota
            s = jnp.where((kpos <= qpos) & (kpos >= lo), r[:, :BQ], masked_fill)
            s_buf[pl.ds(at, BK), :] = s
            p_buf[pl.ds(at, BK), :] = r[:, BQ:]
            return jnp.maximum(mx, jnp.max(s.reshape(BK // 8, 8, BQ), axis=0))

        mx = lax.fori_loop(kb0, kb1, scores_step, jnp.full((8, BQ), masked_fill, f32))
        top = jnp.max(mx, axis=0, keepdims=True)

        def exp_step(kb, sums):
            total, dots = sums
            at = pl.multiple_of(kb * BK, BK)
            e = jnp.exp2((s_buf[pl.ds(at, BK), :] - top) * to_two)
            s_buf[pl.ds(at, BK), :] = e
            w = e * p_buf[pl.ds(at, BK), :]
            return (total + jnp.sum(e.reshape(BK // 8, 8, BQ), axis=0),
                    dots + jnp.sum(w.reshape(BK // 8, 8, BQ), axis=0))

        zeros = jnp.zeros((8, BQ), f32)
        total, dots = lax.fori_loop(kb0, kb1, exp_step, (zeros, zeros))
        inv = 1.0 / jnp.sum(total, axis=0, keepdims=True)
        row_dot = jnp.sum(dots, axis=0, keepdims=True) * inv

        def grad_step(kb, outs):
            dq_t, at_t = outs
            at = pl.multiple_of(kb * BK, BK)
            p = s_buf[pl.ds(at, BK), :] * inv
            ds = p * (p_buf[pl.ds(at, BK), :] - row_dot)
            p_low = p.astype(bf16)
            ds_low = ds.astype(bf16)
            joined = jnp.concatenate([ds_low, p_low], axis=1)
            acc_s[pl.ds(at, BK), :] += mm(joined, both, ((1,), (0,)))
            dq_t = dq_t + mm(kvt_s[0:64, pl.ds(at, BK)], ds_low, ((1,), (0,)))
            at_t = at_t + mm(kvt_s[64:128, pl.ds(at, BK)], p_low, ((1,), (0,)))
            return dq_t, at_t

        wide = jnp.zeros((64, BQ), f32)
        dq_t, at_t = lax.fori_loop(kb0, kb1, grad_step, (wide, wide))
        dq_ref[m, pl.ds(off, BQ), :] = jnp.concatenate([dq_t, at_t], axis=0).T
        return carry

    lax.fori_loop(0, members * per, query_block, 0)

    for m in range(members):
        at_own = pl.multiple_of((2 * m + parity) * rows, rows)
        at_other = pl.multiple_of((2 * m + 1 - parity) * rows, rows)
        own_ref[m] = acc_s[pl.ds(at_own, rows), :]
        send_ref[m] = acc_s[pl.ds(at_other, rows), :]


def attend(scal, lo, x, kv_other):
    members, _, rows, _ = x.shape
    total = 2 * members * rows
    piece = jax.ShapeDtypeStruct((members, rows, 128), f32)
    vmem = pl.BlockSpec(memory_space=pltpu.VMEM)
    return pl.pallas_call(
        attend_kernel,
        in_specs=[pl.BlockSpec(memory_space=pltpu.SMEM), vmem, vmem, vmem],
        out_specs=[vmem, vmem, vmem],
        out_shape=[piece, piece, piece],
        scratch_shapes=[
            pltpu.VMEM((total, 128), bf16),
            pltpu.VMEM((128, total), bf16),
            pltpu.VMEM((total, BQ), f32),
            pltpu.VMEM((total, BQ), f32),
            pltpu.VMEM((total, 128), f32),
        ],
        compiler_params=pltpu.CompilerParams(vmem_limit_bytes=VMEM_LIMIT),
        name="attend",
    )(scal, lo, x, kv_other)


def join_kernel(dq_ref, own_ref, got_ref, c_ref, s_ref, out):
    rows = dq_ref.shape[1]
    lane = lax.broadcasted_iota(jnp.int32, (rows, 128), 1)
    scale = jnp.where(lane < 64, HEAD_DIM ** (-0.5), 1.0)
    cos_tab = c_ref[0]
    sine_tab = -s_ref[0]
    out[0, 0] = turn(dq_ref[0] * scale, cos_tab, sine_tab, lane).astype(bf16)
    out[0, 1] = turn((own_ref[0] + got_ref[0]) * scale, cos_tab, sine_tab, lane).astype(bf16)


def join(dq, own, got, cos_tab, sine_tab):
    members, rows, _ = dq.shape
    one = pl.BlockSpec((1, rows, 128), lambda m: (m, 0, 0))
    return pl.pallas_call(
        join_kernel,
        grid=(members,),
        in_specs=[one] * 5,
        out_specs=pl.BlockSpec((1, 2, rows, 128), lambda m: (m, 0, 0, 0)),
        out_shape=jax.ShapeDtypeStruct((members, 2, rows, 128), bf16),
        name="join",
    )(dq, own, got, cos_tab, sine_tab)


def gather_kernel(scal, x_ref, proj_ref, att_ref):
    members, _, rows, _ = x_ref.shape
    place = scal[0]
    low = lax.broadcasted_iota(jnp.int32, (rows, 128), 1) < 64
    half = members * 64
    for pair in range(members // 2):
        d0 = (place - 2 * pair + members) % members
        d1 = (place - 2 * pair - 1 + members) % members
        for side in range(2):
            a = x_ref[d0, side].astype(f32)
            b = x_ref[d1, side].astype(f32)
            front = jnp.where(low, a, pltpu.roll(b, 64, 1)).astype(bf16)
            back = jnp.where(low, pltpu.roll(a, 64, 1), b).astype(bf16)
            cut = slice(128 * pair, 128 * pair + 128)
            if side == 0:
                proj_ref[:, cut] = front
                att_ref[:, cut] = back
            else:
                proj_ref[:, half + 128 * pair : half + 128 * pair + 128] = front
                proj_ref[:, 2 * half + 128 * pair : 2 * half + 128 * pair + 128] = back


def gather_heads(scal, x):
    members, _, rows, _ = x.shape
    vmem = pl.BlockSpec(memory_space=pltpu.VMEM)
    return pl.pallas_call(
        gather_kernel,
        in_specs=[pl.BlockSpec(memory_space=pltpu.SMEM), vmem],
        out_specs=[vmem, vmem],
        out_shape=[
            jax.ShapeDtypeStruct((rows, 3 * members * 64), bf16),
            jax.ShapeDtypeStruct((rows, members * 64), bf16),
        ],
        compiler_params=pltpu.CompilerParams(vmem_limit_bytes=VMEM_LIMIT),
        name="gather_heads",
    )(scal, x)


def body(inputs, cotangent, doc_lengths, pad_counts, ln_gain, ln_bias,
         w_first, b_first, w_second, b_second):
    rows = inputs.shape[0]
    count = lax.axis_size("seq")
    span = SEQ_LEN // rows
    lead = span // 2
    members = span // 2
    half = members * HEAD_DIM
    half_ff = FF // 2
    seq_at = lax.axis_index("seq")
    branch = lax.axis_index("pair")
    on_first = branch == 0
    block_at = (seq_at - lead) % count
    seq_no = block_at // span
    block_in = block_at % span
    place = block_in // 2
    parity = block_in % 2

    def device_of(block):
        return (block + lead) % count

    def seq_swap(bit):
        return [(i, i ^ bit) for i in range(count)]

    core_swap = [(device_of(b), device_of(b ^ 1)) for b in range(count)]

    weights = w_first[0]
    ids = jnp.arange(rows, dtype=jnp.int32)

    widened = inputs.astype(f32)
    centred = widened - jnp.mean(widened, axis=1, keepdims=True)
    rstd = lax.rsqrt(jnp.mean(centred * centred, axis=1, keepdims=True) + epsilon)
    hidden = (centred * rstd * ln_gain + ln_bias).astype(bf16)

    core = parity
    wu_send = lax.dynamic_slice(weights[:, :half_ff], (core * (D // 2), 0), (D // 2, half_ff))
    wu_got = lax.ppermute(wu_send, ("seq", "pair"), [(2 * i + 1, 2 * i) for i in range(count)])
    b_other = lax.ppermute(b_first, "pair", [(0, 1), (1, 0)])

    cos_q, sine_q = rotation_tables(block_in * rows + ids, 64)
    heads = project(hidden, cotangent, weights, b_first, cos_q, sine_q)
    received = []
    for step in range(members):
        target = (place + step) % members
        got = []
        for side in range(2):
            chunk = lax.dynamic_index_in_dim(heads, side * members + target, 0, keepdims=False)
            route = []
            for b in range(count):
                base, j = b // span * span, b % span
                to = base + (j + 2 * step) % span
                route.append((2 * device_of(b), 2 * device_of(to) + side))
            if step == 0 and side == 0:
                got.append(chunk)
            else:
                got.append(lax.ppermute(chunk, ("seq", "pair"), route))
        received.append(jnp.where(on_first, got[0], got[1]))
    own = jnp.stack(received)
    kv_other = lax.ppermute(own[:, 1], "seq", core_swap)

    def attn_half(matrix, index):
        parts = [matrix[:, j * D + index * half : j * D + index * half + half] for j in range(3)]
        return jnp.concatenate(parts, axis=1)

    held, tied = lax.optimization_barrier((weights, own[0, 0, :8]))
    qkv_second = attn_half(held, 1)
    out_second = held[half : 2 * half, 3 * D :]
    wa_send = jnp.concatenate(
        [
            lax.dynamic_slice(qkv_second, (core * (D // 2), 0), (D // 2, 3 * half)),
            lax.dynamic_slice(out_second, (0, core * (D // 2)), (half, D // 2)),
        ],
        axis=1,
    )
    wa_got = lax.ppermute(wa_send, ("seq", "pair"), [(2 * i, 2 * i + 1) for i in range(count)])

    def both_cores(got):
        other = lax.ppermute(got, "seq", core_swap)
        return (jnp.where(core == 0, got, other), jnp.where(core == 0, other, got))

    wu_low, wu_high = both_cores(wu_got)
    w_up = jnp.where(on_first, jnp.concatenate([wu_low, wu_high], axis=0), weights[:, half_ff:])
    b_up = jnp.where(on_first, b_other[0, :half_ff], b_first[0, half_ff:])
    w_down = lax.dynamic_slice(w_second, (branch * half_ff, 0), (half_ff, D))

    root_half = 0.7071067811865476
    up_proj = mm(hidden, w_up, ((1,), (0,))) + b_up
    cdf = 0.5 * (1.0 + lax.erf(up_proj * root_half))
    active = (up_proj * cdf).astype(bf16)
    slope = cdf + up_proj * jnp.exp(up_proj * up_proj * -0.5) * 0.3989422804014327
    d_active = mm(cotangent, w_down, ((1,), (1,)))
    d_up = (d_active * slope).astype(bf16)
    feed_out = mm(active, w_down, ((1,), (0,)))
    d_hidden_feed = mm(d_up, w_up, ((1,), (1,)))
    g_up = mm(hidden, d_up, ((0,), (0,))).astype(bf16)
    g_down = mm(active, cotangent, ((0,), (0,))).astype(bf16)
    up_bias = jnp.sum(d_up, axis=0, dtype=f32)

    bits = [b for b in range(count.bit_length() - 1)]
    path_one = [bits[0]] + bits[1:]
    path_two = [bits[0]] + bits[2:] + [bits[1]]

    def reduce_scatter(array, path):
        for b in path:
            n, size, cols = array.shape
            bit = (seq_at >> b) & 1
            split = array.reshape(n, 2, size // 2, cols)
            keep = lax.dynamic_index_in_dim(split, bit, 1, keepdims=False)
            send = lax.dynamic_index_in_dim(split, 1 - bit, 1, keepdims=False)
            got = lax.ppermute(send, "seq", seq_swap(1 << b))
            array = (keep.astype(f32) + got.astype(f32)).astype(bf16)
        return array

    def all_gather(array, path):
        for b in reversed(path):
            bit = (seq_at >> b) & 1
            got = lax.ppermute(array, "seq", seq_swap(1 << b))
            array = jnp.where(
                bit == 0,
                jnp.concatenate([array, got], axis=1),
                jnp.concatenate([got, array], axis=1),
            )
        return array

    feed_one = reduce_scatter(jnp.stack([g_up[:, :D], g_down[:D]]), path_one)
    feed_two = reduce_scatter(jnp.stack([g_up[:, D:], g_down[D:]]), path_two)
    down_one = all_gather(feed_one[1:], path_one)
    down_two = all_gather(feed_two[1:], path_two)
    d_w_second = jnp.concatenate([down_one[0], down_two[0]], axis=0).astype(f32)

    doc_row = lax.dynamic_index_in_dim(doc_lengths, seq_no, 0, keepdims=False)
    pads = lax.dynamic_index_in_dim(pad_counts, seq_no, 0, keepdims=False)
    bounds = jnp.cumsum(doc_row)
    own_blocks = 2 * jnp.arange(members, dtype=jnp.int32) + parity
    own_pos = (own_blocks[:, None] * rows + ids[None, :]).reshape(-1)
    start = jnp.max(jnp.where(bounds[:, None] <= own_pos[None, :], bounds[:, None], 0), axis=0)
    lo = jnp.where(own_pos >= SEQ_LEN - pads, own_pos, start)
    lo = lo.reshape(-1, BQ)
    scal = jnp.concatenate([jnp.stack([place, parity]), lo[:, 0]]).astype(jnp.int32)
    dq, dkv_own, dkv_send = attend(scal, lo, own, kv_other)
    dkv_got = lax.ppermute(dkv_send, "seq", core_swap)
    cos_k, sine_k = rotation_tables(own_pos, 128)
    shape_tab = (members, rows, 128)
    back = join(dq, dkv_own, dkv_got, cos_k.reshape(shape_tab), sine_k.reshape(shape_tab))
    returned = []
    for step in range(members):
        target = (place + step) % members
        chunk = lax.dynamic_index_in_dim(back, target, 0, keepdims=False)
        route = []
        for b in range(count):
            base, j = b // span * span, b % span
            route.append((device_of(b), device_of(base + (j + 2 * step) % span)))
        returned.append(chunk if step == 0 else lax.ppermute(chunk, "seq", route))
    d_proj, attended = gather_heads(scal, jnp.stack(returned))

    wa_low, wa_high = both_cores(wa_got)
    w_qkv = jnp.where(
        on_first,
        attn_half(weights, 0),
        jnp.concatenate([wa_low[:, : 3 * half], wa_high[:, : 3 * half]], axis=0),
    )
    w_out = jnp.where(
        on_first,
        weights[:half, 3 * D :],
        jnp.concatenate([wa_low[:, 3 * half :], wa_high[:, 3 * half :]], axis=1),
    )

    g_qkv = mm(hidden, d_proj, ((0,), (0,))).astype(bf16)
    g_out = mm(attended, cotangent, ((0,), (0,))).astype(bf16)
    d_hidden = mm(d_proj, w_qkv, ((1,), (1,))) + d_hidden_feed
    out_part = mm(attended, w_out, ((1,), (0,))) + feed_out
    out_part = out_part + jnp.where(on_first, b_first[0, 3 * D :], 0.0)
    d_hidden_low = d_hidden.astype(bf16)
    out_low = out_part.astype(bf16)
    crossed = lax.ppermute(jnp.stack([out_low, d_hidden_low]), "pair", [(0, 1), (1, 0)])

    packed = g_out.reshape(count, half // count, 2, D // 2)
    packed = packed.transpose(0, 2, 1, 3).reshape(D, D // 2)
    attn_one = reduce_scatter(g_qkv[None, :, :D], path_one)
    attn_two = reduce_scatter(jnp.concatenate([g_qkv[:, D:], packed], axis=1)[None], path_two)

    def slot_shards(attn, feed):
        mine = jnp.where(on_first, attn[0], feed[0])
        other = lax.ppermute(jnp.where(on_first, feed[0], attn[0]), "pair", [(0, 1), (1, 0)])
        return jnp.stack([jnp.where(on_first, mine, other), jnp.where(on_first, other, mine)])

    full_one = all_gather(slot_shards(attn_one, feed_one), path_one)
    full_two = all_gather(slot_shards(attn_two, feed_two), path_two)
    unpacked = full_two[:, :, D // 2 :].reshape(2, count, 2, half // count, D // 2)
    unpacked = unpacked.transpose(0, 1, 3, 2, 4).reshape(D, D)
    as_attn = jnp.concatenate(
        [
            full_one[0, :, :half], full_one[1, :, :half],
            full_one[0, :, half:], full_one[1, :, half:],
            full_two[0, :, :half], full_two[1, :, :half],
            unpacked,
        ],
        axis=1,
    )
    as_feed = jnp.concatenate([full_one[0], full_two[0], full_one[1], full_two[1]], axis=1)
    d_w_first = jnp.where(on_first, as_attn, as_feed).astype(f32)

    outputs = (widened + b_second + (out_low.astype(f32) + crossed[0].astype(f32))).astype(bf16)
    normal = centred * rstd
    e = (d_hidden_low.astype(f32) + crossed[1].astype(f32)) * ln_gain
    d_norm = rstd * (
        e
        - jnp.mean(e, axis=1, keepdims=True)
        - normal * jnp.mean(e * normal, axis=1, keepdims=True)
    )
    d_inputs = (cotangent.astype(f32) + d_norm).astype(bf16)

    def in_half(vector):
        zero = jnp.zeros_like(vector)
        return jnp.stack([jnp.where(on_first, vector, zero), jnp.where(on_first, zero, vector)])

    qkv_bias = jnp.sum(d_proj, axis=0, dtype=f32).reshape(3, half)
    cot_sum = jnp.where(on_first, jnp.sum(cotangent, axis=0, dtype=f32), 0.0)
    small = jnp.concatenate(
        [
            in_half(qkv_bias).transpose(1, 0, 2).reshape(-1),
            in_half(up_bias).reshape(-1),
            cot_sum,
            jnp.sum(d_hidden * normal, axis=0),
            jnp.sum(d_hidden, axis=0),
        ]
    ).reshape(-1, 128)
    for b in bits:
        small = small + lax.ppermute(small, "seq", seq_swap(1 << b))
    small = (small + lax.ppermute(small, "pair", [(0, 1), (1, 0)])).reshape(-1)
    cot_total = small[3 * D + FF : 4 * D + FF]
    d_b_first = jnp.where(
        on_first, jnp.concatenate([small[: 3 * D], cot_total]), small[3 * D : 3 * D + FF]
    )
    return (
        outputs,
        d_inputs,
        small[4 * D + FF : 5 * D + FF],
        small[5 * D + FF :],
        d_w_first[None],
        d_b_first[None],
        d_w_second,
        cot_total,
    )


def solution(mesh):
    in_specs = (
        P("seq", None),
        P("seq", None),
        P(),
        P(),
        P(),
        P(),
        P("pair", None, None),
        P("pair", None),
        P(),
        P(),
    )
    out_specs = (
        P("seq", None),
        P("seq", None),
        P(),
        P(),
        P("pair", None, None),
        P("pair", None),
        P("pair", None),
        P(),
    )
    return jax.shard_map(body, mesh=mesh, in_specs=in_specs, out_specs=out_specs, check_vma=False)
```

```python
import functools

import jax
import jax.numpy as jnp
from jax import lax
from jax.experimental import pallas as pl
from jax.experimental.pallas import tpu as pltpu
from jax.sharding import PartitionSpec as P

HEADS = 16
HEAD_DIM = 64
D = 1024
FF = 4096
ROT = 16
SEQ_LEN = 8192
DOCS = 8
MOST_DOC = 4096

BQ = 512
BK = 512
epsilon = 1e-05
masked_fill = -1e30
bf16 = jnp.bfloat16
f32 = jnp.float32
VMEM_LIMIT = 60 * 1024 * 1024


def after(array, *others):
    return lax.optimization_barrier((array,) + others)[0]


def mm(left, right, dims):
    return lax.dot_general(left, right, (dims, ((), ())), preferred_element_type=f32)


def rotation_tables(positions, period):
    lane = lax.broadcasted_iota(jnp.int32, (positions.shape[0], 128), 1) % period
    inverse = 10000.0 ** (-2.0 * (lane % (ROT // 2)).astype(f32) / ROT)
    angle = positions.astype(f32)[:, None] * inverse
    cos_tab = jnp.where(lane < ROT, jnp.cos(angle), 1.0)
    sine = jnp.sin(angle)
    sine_tab = jnp.where(lane < ROT // 2, -sine, jnp.where(lane < ROT, sine, 0.0))
    return cos_tab, sine_tab


def turn(block, cos_tab, sine_tab, lane):
    from_left = pltpu.roll(block, 8, 1)
    from_right = pltpu.roll(block, 120, 1)
    return block * cos_tab + jnp.where(lane % 64 < 8, from_right, from_left) * sine_tab


def project_kernel(turned, x_ref, y_ref, wx, wy, bx, by, c_ref, s_ref, out):
    rows = x_ref.shape[0]
    lane = lax.broadcasted_iota(jnp.int32, (rows, 128), 1)
    low = lane < 64
    front_all = mm(x_ref[...], wx[...], ((1,), (0,))) + bx[...]
    back_all = mm(y_ref[...], wy[...], ((1,), (1 if turned else 0,))) + by[...]
    cos_tab = c_ref[...]
    sine_tab = s_ref[...]
    for pair in range(wx.shape[1] // 128):
        cut = slice(128 * pair, 128 * pair + 128)
        front = turn(front_all[:, cut], cos_tab, sine_tab, lane)
        back = back_all[:, cut]
        out[2 * pair] = jnp.where(low, front, pltpu.roll(back, 64, 1)).astype(bf16)
        out[2 * pair + 1] = jnp.where(low, pltpu.roll(front, 64, 1), back).astype(bf16)


def project(left, right, w_left, w_right, b_left, b_right, cos_tab, sine_tab, turned):
    rows = left.shape[0]
    heads = w_left.shape[1] // HEAD_DIM
    whole = lambda i: (0, 0)
    part = lambda i: (0, i)
    if turned:
        right_spec = pl.BlockSpec((256, D), lambda i: (i, 0))
    else:
        right_spec = pl.BlockSpec((D, 256), part)
    return pl.pallas_call(
        functools.partial(project_kernel, turned),
        grid=(heads // 4,),
        in_specs=[
            pl.BlockSpec((rows, D), whole),
            pl.BlockSpec((rows, D), whole),
            pl.BlockSpec((D, 256), part),
            right_spec,
            pl.BlockSpec((1, 256), part),
            pl.BlockSpec((1, 256), part),
            pl.BlockSpec((rows, 128), whole),
            pl.BlockSpec((rows, 128), whole),
        ],
        out_specs=pl.BlockSpec((4, rows, 128), lambda i: (i, 0, 0)),
        out_shape=jax.ShapeDtypeStruct((heads, rows, 128), bf16),
        compiler_params=pltpu.CompilerParams(vmem_limit_bytes=VMEM_LIMIT),
        name="project_q" if turned else "project_kv",
    )(left, right, w_left, w_right, b_left[None], b_right[None], cos_tab, sine_tab)


def feed_grad_kernel(orders, h_ref, u_ref, a_ref, g_ref, out):
    step = pl.program_id(0)
    size = out.shape[2]

    for part in range(4):
        @pl.when(step == part)
        def _():
            left, right = (h_ref, u_ref) if part < 2 else (a_ref, g_ref)
            total = mm(left[...], right[...], ((0,), (0,))).astype(bf16)
            order = orders[part] if part < 2 else range(out.shape[0])
            for i, block in enumerate(order):
                out[i, 0] = total[block * size : block * size + size]


def feed_grads(hidden, d_up, active, cotangent, orders):
    rows = hidden.shape[0]
    count = len(orders[0])
    whole = lambda i: (0, 0)
    return pl.pallas_call(
        functools.partial(feed_grad_kernel, orders),
        grid=(4,),
        in_specs=[
            pl.BlockSpec((rows, D), whole),
            pl.BlockSpec((rows, D), lambda i: (0, jnp.minimum(i, 1))),
            pl.BlockSpec((rows, D), lambda i: (0, jnp.maximum(i - 2, 0))),
            pl.BlockSpec((rows, D), whole),
        ],
        out_specs=pl.BlockSpec((count, 1, D // count, D), lambda i: (0, i, 0, 0)),
        out_shape=jax.ShapeDtypeStruct((count, 4, D // count, D), bf16),
        compiler_params=pltpu.CompilerParams(vmem_limit_bytes=VMEM_LIMIT),
        name="feed_grads",
    )(hidden, d_up, active, cotangent)


def attend_kernel(scal, lo_ref, qd_ref, kv_ref, kvp_ref, dq_ref, own_ref, send_ref,
                  kv_s, kvt_s, s_buf, p_buf, acc_s):
    members, rows, _ = qd_ref.shape
    parity = scal[0]
    scale = HEAD_DIM ** (-0.5)
    to_two = scale * 1.4426950408889634

    for m in range(members):
        at_own = pl.multiple_of((2 * m + parity) * rows, rows)
        at_other = pl.multiple_of((2 * m + 1 - parity) * rows, rows)
        kv_s[pl.ds(at_own, rows), :] = kv_ref[m]
        kv_s[pl.ds(at_other, rows), :] = kvp_ref[m]
    acc_s[...] = jnp.zeros_like(acc_s)

    def transpose_step(b, carry):
        at = pl.multiple_of(b * 256, 256)
        kvt_s[:, pl.ds(at, 256)] = kv_s[pl.ds(at, 256), :].astype(f32).T.astype(bf16)
        return carry

    lax.fori_loop(0, kv_s.shape[0] // 256, transpose_step, 0)

    per = rows // BQ
    lane = lax.broadcasted_iota(jnp.int32, (BQ, 128), 1)
    key_iota = lax.broadcasted_iota(jnp.int32, (BK, BQ), 0)
    query_iota = lax.broadcasted_iota(jnp.int32, (1, BQ), 1)

    def query_block(i, carry):
        m = i // per
        part = i % per
        off = pl.multiple_of(part * BQ, BQ)
        first = (2 * m + parity) * rows + off
        qd = qd_ref[m, pl.ds(off, BQ), :]
        zero = jnp.zeros_like(qd)
        qz = jnp.where(lane < 64, qd, zero)
        dz = jnp.where(lane < 64, zero, qd)
        both = jnp.concatenate([qz, dz], axis=0)
        kb0 = scal[1 + i] // BK
        kb1 = (first + BQ - 1) // BK + 1
        qpos = first + query_iota
        lo = lo_ref[pl.ds(i, 1), :]

        def scores_step(kb, mx):
            at = pl.multiple_of(kb * BK, BK)
            r = mm(kv_s[pl.ds(at, BK), :], both, ((1,), (1,)))
            kpos = at + key_iota
            s = jnp.where((kpos <= qpos) & (kpos >= lo), r[:, :BQ], masked_fill)
            to = pl.multiple_of((kb - kb0) * BK, BK)
            s_buf[pl.ds(to, BK), :] = s
            p_buf[pl.ds(to, BK), :] = r[:, BQ:]
            return jnp.maximum(mx, jnp.max(s.reshape(BK // 8, 8, BQ), axis=0))

        mx = lax.fori_loop(kb0, kb1, scores_step, jnp.full((8, BQ), masked_fill, f32))
        top = jnp.max(mx, axis=0, keepdims=True)

        def exp_step(kb, sums):
            total, dots = sums
            at = pl.multiple_of((kb - kb0) * BK, BK)
            e = jnp.exp2((s_buf[pl.ds(at, BK), :] - top) * to_two)
            s_buf[pl.ds(at, BK), :] = e
            w = e * p_buf[pl.ds(at, BK), :]
            return (total + jnp.sum(e.reshape(BK // 8, 8, BQ), axis=0),
                    dots + jnp.sum(w.reshape(BK // 8, 8, BQ), axis=0))

        zeros = jnp.zeros((8, BQ), f32)
        total, dots = lax.fori_loop(kb0, kb1, exp_step, (zeros, zeros))
        inv = 1.0 / jnp.sum(total, axis=0, keepdims=True)
        row_dot = jnp.sum(dots, axis=0, keepdims=True) * inv

        def grad_step(kb, outs):
            dq_t, at_t = outs
            at = pl.multiple_of(kb * BK, BK)
            to = pl.multiple_of((kb - kb0) * BK, BK)
            p = s_buf[pl.ds(to, BK), :] * inv
            ds = p * (p_buf[pl.ds(to, BK), :] - row_dot)
            p_low = p.astype(bf16)
            ds_low = ds.astype(bf16)
            joined = jnp.concatenate([ds_low, p_low], axis=1)
            acc_s[pl.ds(at, BK), :] += mm(joined, both, ((1,), (0,)))
            dq_t = dq_t + mm(kvt_s[0:64, pl.ds(at, BK)], ds_low, ((1,), (0,)))
            at_t = at_t + mm(kvt_s[64:128, pl.ds(at, BK)], p_low, ((1,), (0,)))
            return dq_t, at_t

        wide = jnp.zeros((64, BQ), f32)
        dq_t, at_t = lax.fori_loop(kb0, kb1, grad_step, (wide, wide))
        done = jnp.concatenate([dq_t * scale, at_t], axis=0).T
        dq_ref[m, pl.ds(off, BQ), :] = done.astype(bf16)
        return carry

    lax.fori_loop(0, members * per, query_block, 0)

    for m in range(members):
        at_own = pl.multiple_of((2 * m + parity) * rows, rows)
        at_other = pl.multiple_of((2 * m + 1 - parity) * rows, rows)
        own_ref[m] = acc_s[pl.ds(at_own, rows), :]
        send_ref[m] = acc_s[pl.ds(at_other, rows), :]


def attend(scal, lo, qd, kv, kv_other):
    members, rows, _ = qd.shape
    total = 2 * members * rows
    piece = jax.ShapeDtypeStruct((members, rows, 128), f32)
    vmem = pl.BlockSpec(memory_space=pltpu.VMEM)
    return pl.pallas_call(
        attend_kernel,
        in_specs=[pl.BlockSpec(memory_space=pltpu.SMEM)] + [vmem] * 4,
        out_specs=[vmem, vmem, vmem],
        out_shape=[jax.ShapeDtypeStruct((members, rows, 128), bf16), piece, piece],
        scratch_shapes=[
            pltpu.VMEM((total, 128), bf16),
            pltpu.VMEM((128, total), bf16),
            pltpu.VMEM((MOST_DOC + BQ + BK, BQ), f32),
            pltpu.VMEM((MOST_DOC + BQ + BK, BQ), f32),
            pltpu.VMEM((total, 128), f32),
        ],
        compiler_params=pltpu.CompilerParams(vmem_limit_bytes=VMEM_LIMIT),
        cost_estimate=pl.CostEstimate(
            flops=1_000_000_000_000, transcendentals=10_000_000, bytes_accessed=20_000_000
        ),
        name="attend",
    )(scal, lo, qd, kv, kv_other)


def join_kernel(own_ref, got_ref, out):
    lane = lax.broadcasted_iota(jnp.int32, own_ref.shape, 2)
    scale = jnp.where(lane < 64, HEAD_DIM ** (-0.5), 1.0)
    out[...] = ((own_ref[...] + got_ref[...]) * scale).astype(bf16)


def join(own, got):
    members, rows, _ = own.shape
    two = pl.BlockSpec((2, rows, 128), lambda m: (m, 0, 0))
    return pl.pallas_call(
        join_kernel,
        grid=(members // 2,),
        in_specs=[two] * 2,
        out_specs=two,
        out_shape=jax.ShapeDtypeStruct((members, rows, 128), bf16),
        name="join",
    )(own, got)


def side_by_side(x_ref, c_ref, s_ref, front_ref, back_ref):
    members, rows, _ = x_ref.shape
    lane = lax.broadcasted_iota(jnp.int32, (rows, 128), 1)
    low = lane < 64
    cos_tab = c_ref[...]
    sine_tab = -s_ref[...]
    for pair in range(members // 2):
        a = x_ref[2 * pair].astype(f32)
        b = x_ref[2 * pair + 1].astype(f32)
        cut = slice(128 * pair, 128 * pair + 128)
        front = jnp.where(low, a, pltpu.roll(b, 64, 1))
        front_ref[:, cut] = turn(front, cos_tab, sine_tab, lane).astype(bf16)
        back_ref[:, cut] = jnp.where(low, pltpu.roll(a, 64, 1), b).astype(bf16)


def query_grad_kernel(share, x_ref, c_ref, s_ref, h_ref, g_ref, dq_ref, att_ref, out):
    side_by_side(x_ref, c_ref, s_ref, dq_ref, att_ref)
    half = dq_ref.shape[1]
    out[:, :half] = mm(h_ref[...], dq_ref[...], ((0,), (0,))).astype(bf16)
    g_out = mm(att_ref[...], g_ref[...], ((0,), (0,))).astype(bf16)
    for i in range(half // share):
        rows = slice(i * share, (i + 1) * share)
        out[2 * i * share : (2 * i + 1) * share, half:] = g_out[rows, : D // 2]
        out[(2 * i + 1) * share : (2 * i + 2) * share, half:] = g_out[rows, D // 2 :]


def query_plain_kernel(x_ref, c_ref, s_ref, dq_ref, att_ref):
    side_by_side(x_ref, c_ref, s_ref, dq_ref, att_ref)


def query_grads(x, cos_tab, sine_tab, hidden, cotangent, share):
    members, rows, _ = x.shape
    half = members * HEAD_DIM
    vmem = pl.BlockSpec(memory_space=pltpu.VMEM)
    flat = jax.ShapeDtypeStruct((rows, half), bf16)
    params = pltpu.CompilerParams(vmem_limit_bytes=VMEM_LIMIT)
    if share % 32 == 0:
        return pl.pallas_call(
            functools.partial(query_grad_kernel, share),
            in_specs=[vmem] * 5,
            out_specs=[vmem] * 3,
            out_shape=[flat, flat, jax.ShapeDtypeStruct((D, D), bf16)],
            compiler_params=params,
            name="query_grads",
        )(x, cos_tab, sine_tab, hidden, cotangent)
    d_query, attended = pl.pallas_call(
        query_plain_kernel,
        in_specs=[vmem] * 3,
        out_specs=[vmem] * 2,
        out_shape=[flat, flat],
        compiler_params=params,
        name="query_plain",
    )(x, cos_tab, sine_tab)
    g_query = mm(hidden, d_query, ((0,), (0,))).astype(bf16)
    g_out = mm(attended, cotangent, ((0,), (0,))).astype(bf16)
    packed = g_out.reshape(half // share, share, 2, D // 2).transpose(0, 2, 1, 3)
    return d_query, attended, jnp.concatenate([g_query, packed.reshape(D, D // 2)], axis=1)


def key_grad_kernel(x_ref, c_ref, s_ref, h_ref, dkv_ref, out):
    half = dkv_ref.shape[1] // 2
    side_by_side(x_ref, c_ref, s_ref, dkv_ref.at[:, :half], dkv_ref.at[:, half:])
    out[...] = mm(h_ref[...], dkv_ref[...], ((0,), (0,))).astype(bf16)


def key_grads(x, cos_tab, sine_tab, hidden):
    members, rows, _ = x.shape
    vmem = pl.BlockSpec(memory_space=pltpu.VMEM)
    return pl.pallas_call(
        key_grad_kernel,
        in_specs=[vmem] * 4,
        out_specs=[vmem, vmem],
        out_shape=[
            jax.ShapeDtypeStruct((rows, 2 * members * HEAD_DIM), bf16),
            jax.ShapeDtypeStruct((D, D), bf16),
        ],
        compiler_params=pltpu.CompilerParams(vmem_limit_bytes=VMEM_LIMIT),
        name="key_grads",
    )(x, cos_tab, sine_tab, hidden)


def place_kernel(sel, near_one, far_one, near_two, far_two, near_out, far_out, out):
    step = pl.program_id(0)
    rows = out.shape[1]
    half = D // 2
    at = pl.multiple_of(step % 2 * rows, rows)
    take = pl.ds(at, rows)

    def attn_slot(ones, twos):
        for top in range(2):
            for part in range(2):
                first = part * half
                one = ones[top]
                two = twos[top]
                out[top, :, first : first + half] = one[0, part, take, :half].astype(f32)
                first = first + D
                out[top, :, first : first + half] = two[0, part, take, :half].astype(f32)
                first = first + D
                out[top, :, first : first + half] = two[0, part, take, half:].astype(f32)

    def feed_slot(ones, twos):
        for top in range(2):
            for part in range(2):
                first = 2 * part * D
                out[top, :, first : first + D] = ones[top][0, part, take, :].astype(f32)
                first = first + D
                out[top, :, first : first + D] = twos[top][0, part, take, :].astype(f32)

    def last_columns(source):
        for part in range(2):
            for side in range(2):
                first = 3 * D + side * half
                picked = source[0, part, side * rows : side * rows + rows, :]
                out[part, :, first : first + half] = picked.astype(f32)

    for slot, fill in enumerate((attn_slot, feed_slot)):
        for own in range(2):
            @pl.when((sel[0] == slot) & (sel[1] == own))
            def _():
                if own == 0:
                    fill((near_one, far_one), (near_two, far_two))
                else:
                    fill((far_one, near_one), (far_two, near_two))

    use_near = (step < pl.num_programs(0) // 2) == (sel[1] == 0)

    @pl.when((sel[0] == 0) & use_near)
    def _():
        last_columns(near_out)

    @pl.when((sel[0] == 0) & jnp.logical_not(use_near))
    def _():
        last_columns(far_out)


def place_slot(near_one, far_one, near_two, far_two, sel):
    half = near_one.shape[0]
    rows = near_one.shape[2]
    shape = (1, 2, rows, D)

    def by_pair(offset):
        return pl.BlockSpec(shape, lambda i, sel: ((i // 2) ^ sel[offset], 0, 0, 0))

    def out_spec(own):
        def index(i, sel):
            used = (sel[0] == 0) & ((i < half) == (sel[1] == own))
            return (jnp.where(used, (i % half) ^ sel[2], half - 1), 0, 0, 1)

        return pl.BlockSpec((1, 2, rows, D // 2), index)

    placed = pl.pallas_call(
        place_kernel,
        grid_spec=pltpu.PrefetchScalarGridSpec(
            num_scalar_prefetch=1,
            grid=(2 * half,),
            in_specs=[by_pair(2), by_pair(2), by_pair(3), by_pair(3), out_spec(0), out_spec(1)],
            out_specs=pl.BlockSpec((2, rows // 2, FF), lambda i, sel: (0, i, 0)),
        ),
        out_shape=jax.ShapeDtypeStruct((2, D // 2, FF), f32),
        compiler_params=pltpu.CompilerParams(vmem_limit_bytes=VMEM_LIMIT),
        name="place",
    )(sel, near_one, far_one, near_two, far_two, near_one, far_one)
    return placed.reshape(D, FF)


def body(inputs, cotangent, doc_lengths, pad_counts, ln_gain, ln_bias,
         w_first, b_first, w_second, b_second):
    rows = inputs.shape[0]
    count = lax.axis_size("seq")
    span = SEQ_LEN // rows
    lead = span // 2
    members = span // 2
    half = members * HEAD_DIM
    half_ff = FF // 2
    seq_at = lax.axis_index("seq")
    branch = lax.axis_index("pair")
    on_first = branch == 0
    block_at = (seq_at - lead) % count
    seq_no = block_at // span
    block_in = block_at % span
    place = block_in // 2
    parity = block_in % 2

    def device_of(block):
        return (block + lead) % count

    def seq_swap(bit):
        return [(i, i ^ bit) for i in range(count)]

    core_swap = [(device_of(b), device_of(b ^ 1)) for b in range(count)]

    weights = w_first[0]
    ids = jnp.arange(rows, dtype=jnp.int32)

    widened = inputs.astype(f32)
    centred = widened - jnp.mean(widened, axis=1, keepdims=True)
    rstd = lax.rsqrt(jnp.mean(centred * centred, axis=1, keepdims=True) + epsilon)
    hidden = (centred * rstd * ln_gain + ln_bias).astype(bf16)

    core = parity
    half_d = D // 2
    to_second = [(2 * i, 2 * i + 1) for i in range(count)]
    to_first = [(2 * i + 1, 2 * i) for i in range(count)]
    both_ways = [(0, 1), (1, 0)]

    def my_rows(at, width):
        return lax.dynamic_slice(weights, (core * half_d, at), (half_d, width))

    def columns(slot_part, index):
        at = slot_part * D + index * half
        return weights[:, at : at + half]

    def both_cores(got):
        other = lax.ppermute(got, "seq", core_swap)
        return (jnp.where(core == 0, got, other), jnp.where(core == 0, other, got))

    out_second = lax.dynamic_slice(weights, (half, 3 * D + core * half_d), (half, half_d))
    kv_sent = jnp.concatenate([my_rows(j * D + half, half) for j in (1, 2)], axis=1)
    kv_crossed = lax.ppermute(kv_sent, ("seq", "pair"), to_second)
    qo_sent = after(jnp.concatenate([my_rows(half, half), out_second], axis=1), kv_crossed)
    qo_crossed = lax.ppermute(qo_sent, ("seq", "pair"), to_second)
    up_crossed = lax.ppermute(my_rows(0, half_ff), ("seq", "pair"), to_first)
    b_other = lax.ppermute(b_first, "pair", both_ways)
    own_blocks = 2 * jnp.arange(members, dtype=jnp.int32) + parity
    own_pos = (own_blocks[:, None] * rows + ids[None, :]).reshape(-1)
    cos_q, sine_q = rotation_tables(block_in * rows + ids, 64)
    kv_low, kv_high = both_cores(kv_crossed)
    w_kv = jnp.where(
        on_first,
        jnp.concatenate([columns(1, 0), columns(2, 0)], axis=1),
        jnp.concatenate([kv_low, kv_high], axis=0),
    )
    b_attn = jnp.where(on_first, b_first[0], b_other[0])
    b_q, b_k, b_v = (
        lax.dynamic_slice(b_attn, (j * D + branch * half,), (half,)) for j in range(3)
    )
    kv_heads = project(
        hidden, hidden, w_kv[:, :half], w_kv[:, half:], b_k, b_v, cos_q, sine_q, False
    )
    qo_low, qo_high = both_cores(after(qo_crossed, kv_heads))
    w_q = jnp.where(
        on_first, columns(0, 0), jnp.concatenate([qo_low[:, :half], qo_high[:, :half]], axis=0)
    )
    w_out = jnp.where(
        on_first,
        weights[:half, 3 * D :],
        jnp.concatenate([qo_low[:, half:], qo_high[:, half:]], axis=1),
    )

    groups = [
        [device_of(n * span + 2 * m + k) for m in range(members)]
        for n in range(count // span)
        for k in range(2)
    ]

    def spread(blocks):
        return lax.all_to_all(blocks, "seq", 0, 0, axis_index_groups=groups)

    kv_own = spread(kv_heads)
    kv_other = lax.ppermute(kv_own, "seq", core_swap)
    qd_heads = project(
        hidden, cotangent, w_q, w_out, b_q, jnp.zeros_like(b_q), cos_q, sine_q, True
    )
    qd_own = spread(qd_heads)

    bits = list(range(count.bit_length() - 1))
    path_one = list(bits)
    path_two = [bits[0], bits[2], bits[1]] + bits[3:]

    def in_path(index, path):
        moved = [((index >> b) & 1) << (len(path) - 1 - i) for i, b in enumerate(path)]
        return functools.reduce(lambda x, y: x | y, moved)

    up_low, up_high = both_cores(up_crossed)
    w_up = jnp.where(on_first, jnp.concatenate([up_low, up_high], axis=0), weights[:, half_ff:])
    w_up = after(w_up, kv_other, qd_heads)
    b_up = jnp.where(on_first, b_other[0, :half_ff], b_first[0, half_ff:])
    w_down = lax.dynamic_slice(w_second, (branch * half_ff, 0), (half_ff, D))
    root_half = 0.7071067811865476
    up_proj = mm(hidden, w_up, ((1,), (0,))) + b_up
    cdf = 0.5 * (1.0 + lax.erf(up_proj * root_half))
    active = (up_proj * cdf).astype(bf16)
    slope = cdf + up_proj * jnp.exp(up_proj * up_proj * -0.5) * 0.3989422804014327
    d_active = mm(cotangent, w_down, ((1,), (1,)))
    d_up = (d_active * slope).astype(bf16)
    orders = [[in_path(i, path) for i in range(count)] for path in (path_one, path_two)]
    g_feed = feed_grads(hidden, d_up, active, cotangent, orders)
    up_bias = jnp.sum(d_up, axis=0, dtype=f32)
    feed_shard = lax.psum_scatter(g_feed, "seq", scatter_dimension=0, tiled=True)[0]

    def scatter_step(array, b):
        size, cols = array.shape
        bit = (seq_at >> b) & 1
        split = array.reshape(2, size // 2, cols)
        keep = lax.dynamic_index_in_dim(split, bit, 0, keepdims=False)
        send = lax.dynamic_index_in_dim(split, 1 - bit, 0, keepdims=False)
        got = lax.ppermute(send, "seq", seq_swap(1 << b))
        return (keep.astype(f32) + got.astype(f32)).astype(bf16)

    def gather_step(array, b):
        return jnp.concatenate([array, lax.ppermute(array, "seq", seq_swap(1 << b))], axis=0)

    doc_row = lax.dynamic_index_in_dim(doc_lengths, seq_no, 0, keepdims=False)
    pads = lax.dynamic_index_in_dim(pad_counts, seq_no, 0, keepdims=False)
    bounds = jnp.cumsum(doc_row)
    start = jnp.max(jnp.where(bounds[:, None] <= own_pos[None, :], bounds[:, None], 0), axis=0)
    lo = jnp.where(own_pos >= SEQ_LEN - pads, own_pos, start)
    lo = lo.reshape(-1, BQ)
    scal = jnp.concatenate([parity[None], lo[:, 0]]).astype(jnp.int32)
    qd_own = after(qd_own, g_feed)
    dq_att, dkv_own, dkv_send = attend(scal, lo, qd_own, kv_own, kv_other)
    dkv_got = lax.ppermute(dkv_send, "seq", core_swap)
    active = after(active, dq_att)
    d_up = after(d_up, dq_att)
    feed_out = mm(active, w_down, ((1,), (0,)))
    d_hidden_feed = mm(d_up, w_up, ((1,), (1,)))
    dq_att = spread(dq_att)
    d_kv = join(dkv_own, dkv_got)
    dq_att, d_kv, feed_out, d_hidden_feed = lax.optimization_barrier(
        (dq_att, d_kv, feed_out, d_hidden_feed)
    )
    d_kv = spread(d_kv)

    share = half // count
    d_query, attended, g_one = query_grads(dq_att, cos_q, sine_q, hidden, cotangent, share)
    attn_one = scatter_step(scatter_step(g_one, path_one[0]), path_one[1])
    d_hidden = mm(d_query, w_q, ((1,), (1,))) + d_hidden_feed
    out_part = mm(attended, w_out, ((1,), (0,))) + feed_out
    out_low = (out_part + jnp.where(on_first, b_first[0, 3 * D :], 0.0)).astype(bf16)
    d_kv, feed_shard, attn_one, d_hidden, out_low = lax.optimization_barrier(
        (d_kv, feed_shard, attn_one, d_hidden, out_low)
    )
    down_all = lax.all_gather(feed_shard[2:], "seq", axis=0)

    d_keys, g_two = key_grads(d_kv, cos_q, sine_q, hidden)
    d_hidden = d_hidden + mm(d_keys, w_kv, ((1,), (1,)))
    d_hidden_low = d_hidden.astype(bf16)

    def in_half(vector):
        zero = jnp.zeros_like(vector)
        return jnp.stack([jnp.where(on_first, vector, zero), jnp.where(on_first, zero, vector)])

    normal = centred * rstd
    q_bias = jnp.sum(d_query, axis=0, dtype=f32)
    kv_bias = jnp.sum(d_keys, axis=0, dtype=f32)
    qkv_bias = jnp.concatenate([q_bias, kv_bias]).reshape(3, half)
    cot_sum = jnp.where(on_first, jnp.sum(cotangent, axis=0, dtype=f32), 0.0)
    small = jnp.concatenate(
        [
            in_half(qkv_bias).transpose(1, 0, 2).reshape(-1),
            in_half(up_bias).reshape(-1),
            cot_sum,
            jnp.sum(d_hidden * normal, axis=0),
            jnp.sum(d_hidden, axis=0),
        ]
    ).reshape(-1, 128)

    attn_two = g_two
    ahead = list(path_one[2:])
    for i, b in enumerate(path_two):
        if ahead:
            attn_one = scatter_step(attn_one, ahead.pop(0))
        attn_two = scatter_step(attn_two, b)
        attn_one, attn_two = lax.optimization_barrier((attn_one, attn_two))
        if i == 1:
            attn_two, d_hidden_low, small = lax.optimization_barrier(
                (attn_two, d_hidden_low, small)
            )

    attn_both = jnp.stack([attn_one, attn_two])
    feed_both = feed_shard[:2]
    other = lax.ppermute(jnp.where(on_first, feed_both, attn_both), "pair", both_ways)
    zero_slot = jnp.where(on_first, attn_both, other)
    one_slot = jnp.where(on_first, other, feed_both)
    near_one = jnp.stack([zero_slot[0], one_slot[0]])[None]
    near_two = jnp.stack([zero_slot[1], one_slot[1]])[None]
    crossed = after(jnp.stack([out_low, d_hidden_low]), near_one, near_two)
    crossed = lax.ppermute(crossed, "pair", both_ways)
    small = small + lax.ppermute(small, "pair", both_ways)
    for i in range(len(bits) - 1, 0, -1):
        near_one = gather_step(near_one, path_one[i])
        near_two = gather_step(near_two, path_two[i])
        small = small + lax.ppermute(small, "seq", seq_swap(1 << path_two[i]))
        near_one, near_two, small = lax.optimization_barrier((near_one, near_two, small))
        if i == 2:
            crossed, down_all = lax.optimization_barrier((crossed, down_all, near_two))[:2]
    outputs = (widened + b_second + (out_low.astype(f32) + crossed[0].astype(f32))).astype(bf16)
    e = (d_hidden_low.astype(f32) + crossed[1].astype(f32)) * ln_gain
    d_norm = rstd * (
        e
        - jnp.mean(e, axis=1, keepdims=True)
        - normal * jnp.mean(e * normal, axis=1, keepdims=True)
    )
    d_inputs = (cotangent.astype(f32) + d_norm).astype(bf16)

    my_one = in_path(seq_at, path_one)
    my_two = in_path(seq_at, path_two)
    d_w_second = down_all.transpose(1, 0, 2, 3).reshape(half_ff, D).astype(f32)
    near_two, outputs, d_inputs, d_w_second = lax.optimization_barrier(
        (near_two, outputs, d_inputs, d_w_second)
    )
    far_two = lax.ppermute(near_two, "seq", seq_swap(1 << path_two[0]))
    small = small + lax.ppermute(small, "seq", seq_swap(1 << path_two[0]))
    far_one = lax.ppermute(near_one, "seq", seq_swap(1 << path_one[0]))
    small = small.reshape(-1)
    if share % 32 == 0:
        low_bits = count // 2 - 1
        sel = jnp.stack([branch, core, my_one & low_bits, my_two & low_bits]).astype(jnp.int32)
        d_w_first = place_slot(near_one, far_one, near_two, far_two, sel)
    else:
        order = jnp.arange(count, dtype=jnp.int32)
        full_one = jnp.take(jnp.concatenate([near_one, far_one]), order ^ my_one, axis=0)
        full_two = jnp.take(jnp.concatenate([near_two, far_two]), order ^ my_two, axis=0)
        full_one = full_one.transpose(1, 0, 2, 3).reshape(2, D, D)
        full_two = full_two.transpose(1, 0, 2, 3).reshape(2, D, D)
        unpacked = full_one[:, :, half:].reshape(2, count, 2, share, half)
        unpacked = unpacked.transpose(0, 1, 3, 2, 4).reshape(D, D)
        as_attn = jnp.concatenate(
            [
                full_one[0, :, :half], full_one[1, :, :half],
                full_two[0, :, :half], full_two[1, :, :half],
                full_two[0, :, half:], full_two[1, :, half:],
                unpacked,
            ],
            axis=1,
        )
        as_feed = jnp.concatenate([full_one[0], full_two[0], full_one[1], full_two[1]], axis=1)
        d_w_first = jnp.where(on_first, as_attn, as_feed).astype(f32)

    cot_total = small[3 * D + FF : 4 * D + FF]
    d_b_first = jnp.where(
        on_first, jnp.concatenate([small[: 3 * D], cot_total]), small[3 * D : 3 * D + FF]
    )
    return (
        outputs,
        d_inputs,
        small[4 * D + FF : 5 * D + FF],
        small[5 * D + FF :],
        d_w_first[None],
        d_b_first[None],
        d_w_second,
        cot_total,
    )


def solution(mesh):
    in_specs = (
        P("seq", None),
        P("seq", None),
        P(),
        P(),
        P(),
        P(),
        P("pair", None, None),
        P("pair", None),
        P(),
        P(),
    )
    out_specs = (
        P("seq", None),
        P("seq", None),
        P(),
        P(),
        P("pair", None, None),
        P("pair", None),
        P("pair", None),
        P(),
    )
    return jax.shard_map(body, mesh=mesh, in_specs=in_specs, out_specs=out_specs, check_vma=False)
```

```python
import functools

import jax
import jax.numpy as jnp
from jax import lax
from jax.experimental import pallas as pl
from jax.experimental.pallas import tpu as pltpu
from jax.sharding import PartitionSpec as P

HEADS = 16
HEAD_DIM = 64
D = 1024
FF = 4096
ROT = 16
SEQ_LEN = 8192
DOCS = 8
MOST_DOC = 4096

BQ = 512
BK = 512
epsilon = 1e-05
masked_fill = -1e30
bf16 = jnp.bfloat16
f32 = jnp.float32
VMEM_LIMIT = 60 * 1024 * 1024


def after(array, *others):
    return lax.optimization_barrier((array,) + others)[0]


def mm(left, right, dims):
    return lax.dot_general(left, right, (dims, ((), ())), preferred_element_type=f32)


def rotation_tables(positions, period):
    lane = lax.broadcasted_iota(jnp.int32, (positions.shape[0], 128), 1) % period
    inverse = 10000.0 ** (-2.0 * (lane % (ROT // 2)).astype(f32) / ROT)
    angle = positions.astype(f32)[:, None] * inverse
    cos_tab = jnp.where(lane < ROT, jnp.cos(angle), 1.0)
    sine = jnp.sin(angle)
    sine_tab = jnp.where(lane < ROT // 2, -sine, jnp.where(lane < ROT, sine, 0.0))
    return cos_tab, sine_tab


def turn(block, cos_tab, sine_tab, lane):
    from_left = pltpu.roll(block, 8, 1)
    from_right = pltpu.roll(block, 120, 1)
    return block * cos_tab + jnp.where(lane % 64 < 8, from_right, from_left) * sine_tab


def project_kernel(turned, x_ref, y_ref, wx, wy, bx, by, c_ref, s_ref, out):
    rows = x_ref.shape[0]
    lane = lax.broadcasted_iota(jnp.int32, (rows, 128), 1)
    low = lane < 64
    front_all = mm(x_ref[...], wx[...], ((1,), (0,))) + bx[...]
    back_all = mm(y_ref[...], wy[...], ((1,), (1 if turned else 0,))) + by[...]
    cos_tab = c_ref[...]
    sine_tab = s_ref[...]
    for pair in range(wx.shape[1] // 128):
        cut = slice(128 * pair, 128 * pair + 128)
        front = turn(front_all[:, cut], cos_tab, sine_tab, lane)
        back = back_all[:, cut]
        out[2 * pair] = jnp.where(low, front, pltpu.roll(back, 64, 1)).astype(bf16)
        out[2 * pair + 1] = jnp.where(low, pltpu.roll(front, 64, 1), back).astype(bf16)


def project(left, right, w_left, w_right, b_left, b_right, cos_tab, sine_tab, turned):
    rows = left.shape[0]
    heads = w_left.shape[1] // HEAD_DIM
    whole = lambda i: (0, 0)
    part = lambda i: (0, i)
    if turned:
        right_spec = pl.BlockSpec((256, D), lambda i: (i, 0))
    else:
        right_spec = pl.BlockSpec((D, 256), part)
    return pl.pallas_call(
        functools.partial(project_kernel, turned),
        grid=(heads // 4,),
        in_specs=[
            pl.BlockSpec((rows, D), whole),
            pl.BlockSpec((rows, D), whole),
            pl.BlockSpec((D, 256), part),
            right_spec,
            pl.BlockSpec((1, 256), part),
            pl.BlockSpec((1, 256), part),
            pl.BlockSpec((rows, 128), whole),
            pl.BlockSpec((rows, 128), whole),
        ],
        out_specs=pl.BlockSpec((4, rows, 128), lambda i: (i, 0, 0)),
        out_shape=jax.ShapeDtypeStruct((heads, rows, 128), bf16),
        compiler_params=pltpu.CompilerParams(vmem_limit_bytes=VMEM_LIMIT),
        name="project_q" if turned else "project_kv",
    )(left, right, w_left, w_right, b_left[None], b_right[None], cos_tab, sine_tab)


def feed_grad_kernel(orders, h_ref, u_ref, a_ref, g_ref, out):
    step = pl.program_id(0)
    size = out.shape[2]

    for part in range(4):
        @pl.when(step == part)
        def _():
            left, right = (h_ref, u_ref) if part < 2 else (a_ref, g_ref)
            total = mm(left[...], right[...], ((0,), (0,))).astype(bf16)
            order = orders[part] if part < 2 else range(out.shape[0])
            for i, block in enumerate(order):
                out[i, 0] = total[block * size : block * size + size]


def feed_grads(hidden, d_up, active, cotangent, orders):
    rows = hidden.shape[0]
    count = len(orders[0])
    whole = lambda i: (0, 0)
    return pl.pallas_call(
        functools.partial(feed_grad_kernel, orders),
        grid=(4,),
        in_specs=[
            pl.BlockSpec((rows, D), whole),
            pl.BlockSpec((rows, D), lambda i: (0, jnp.minimum(i, 1))),
            pl.BlockSpec((rows, D), lambda i: (0, jnp.maximum(i - 2, 0))),
            pl.BlockSpec((rows, D), whole),
        ],
        out_specs=pl.BlockSpec((count, 1, D // count, D), lambda i: (0, i, 0, 0)),
        out_shape=jax.ShapeDtypeStruct((count, 4, D // count, D), bf16),
        compiler_params=pltpu.CompilerParams(vmem_limit_bytes=VMEM_LIMIT),
        name="feed_grads",
    )(hidden, d_up, active, cotangent)


def attend_kernel(scal, lo_ref, qd_ref, kv_ref, kvp_ref, dq_ref, own_ref, send_ref,
                  kv_s, kvt_s, s_buf, p_buf, acc_s, m_s):
    members, rows, _ = qd_ref.shape
    parity = scal[0]
    scale = HEAD_DIM ** (-0.5)
    to_two = scale * 1.4426950408889634

    for m in range(members):
        at_own = pl.multiple_of((2 * m + parity) * rows, rows)
        at_other = pl.multiple_of((2 * m + 1 - parity) * rows, rows)
        kv_s[pl.ds(at_own, rows), :] = kv_ref[m]
        kv_s[pl.ds(at_other, rows), :] = kvp_ref[m]
    acc_s[...] = jnp.zeros_like(acc_s)

    def transpose_step(b, carry):
        at = pl.multiple_of(b * 256, 256)
        kvt_s[:, pl.ds(at, 256)] = kv_s[pl.ds(at, 256), :].astype(f32).T.astype(bf16)
        return carry

    lax.fori_loop(0, kv_s.shape[0] // 256, transpose_step, 0)

    per = rows // BQ
    lane = lax.broadcasted_iota(jnp.int32, (BQ, 128), 1)
    key_iota = lax.broadcasted_iota(jnp.int32, (BK, BQ), 0)
    query_iota = lax.broadcasted_iota(jnp.int32, (1, BQ), 1)

    def query_block(i, carry):
        m = i // per
        part = i % per
        off = pl.multiple_of(part * BQ, BQ)
        first = (2 * m + parity) * rows + off
        qd = qd_ref[m, pl.ds(off, BQ), :]
        zero = jnp.zeros_like(qd)
        qz = jnp.where(lane < 64, qd, zero)
        dz = jnp.where(lane < 64, zero, qd)
        both = jnp.concatenate([qz, dz], axis=0)
        kb0 = scal[1 + i] // BK
        kb1 = (first + BQ - 1) // BK + 1
        qpos = first + query_iota
        lo = lo_ref[pl.ds(i, 1), :]

        def scores_step(kb, sums):
            top, total, dots = sums
            at = pl.multiple_of(kb * BK, BK)
            r = mm(kv_s[pl.ds(at, BK), :], both, ((1,), (1,)))
            kpos = at + key_iota
            s = jnp.where((kpos <= qpos) & (kpos >= lo), r[:, :BQ], masked_fill)
            eights = jnp.max(s.reshape(BK // 8, 8, BQ), axis=0)
            new_top = jnp.maximum(top, jnp.max(eights, axis=0, keepdims=True))
            e = jnp.exp2((s - new_top) * to_two)
            w = e * r[:, BQ:]
            to = pl.multiple_of((kb - kb0) * BK, BK)
            s_buf[pl.ds(to, BK), :] = e
            p_buf[pl.ds(to, BK), :] = r[:, BQ:]
            m_s[pl.ds(kb - kb0, 1), :] = new_top
            shrink = jnp.exp2((top - new_top) * to_two)
            return (new_top,
                    total * shrink + jnp.sum(e.reshape(BK // 8, 8, BQ), axis=0),
                    dots * shrink + jnp.sum(w.reshape(BK // 8, 8, BQ), axis=0))

        zeros = jnp.zeros((8, BQ), f32)
        lowest = jnp.full((1, BQ), masked_fill, f32)
        top, total, dots = lax.fori_loop(kb0, kb1, scores_step, (lowest, zeros, zeros))
        inv = 1.0 / jnp.sum(total, axis=0, keepdims=True)
        row_dot = jnp.sum(dots, axis=0, keepdims=True) * inv

        def grad_step(kb, outs):
            dq_t, at_t = outs
            at = pl.multiple_of(kb * BK, BK)
            to = pl.multiple_of((kb - kb0) * BK, BK)
            share = jnp.exp2((m_s[pl.ds(kb - kb0, 1), :] - top) * to_two) * inv
            p = s_buf[pl.ds(to, BK), :] * share
            ds = p * (p_buf[pl.ds(to, BK), :] - row_dot)
            p_low = p.astype(bf16)
            ds_low = ds.astype(bf16)
            joined = jnp.concatenate([ds_low, p_low], axis=1)
            acc_s[pl.ds(at, BK), :] += mm(joined, both, ((1,), (0,)))
            dq_t = dq_t + mm(kvt_s[0:64, pl.ds(at, BK)], ds_low, ((1,), (0,)))
            at_t = at_t + mm(kvt_s[64:128, pl.ds(at, BK)], p_low, ((1,), (0,)))
            return dq_t, at_t

        wide = jnp.zeros((64, BQ), f32)
        dq_t, at_t = lax.fori_loop(kb0, kb1, grad_step, (wide, wide))
        done = jnp.concatenate([dq_t * scale, at_t], axis=0).T
        dq_ref[m, pl.ds(off, BQ), :] = done.astype(bf16)
        return carry

    lax.fori_loop(0, members * per, query_block, 0)

    for m in range(members):
        at_own = pl.multiple_of((2 * m + parity) * rows, rows)
        at_other = pl.multiple_of((2 * m + 1 - parity) * rows, rows)
        own_ref[m] = acc_s[pl.ds(at_own, rows), :]
        send_ref[m] = acc_s[pl.ds(at_other, rows), :]


def attend(scal, lo, qd, kv, kv_other):
    members, rows, _ = qd.shape
    total = 2 * members * rows
    piece = jax.ShapeDtypeStruct((members, rows, 128), f32)
    vmem = pl.BlockSpec(memory_space=pltpu.VMEM)
    return pl.pallas_call(
        attend_kernel,
        in_specs=[pl.BlockSpec(memory_space=pltpu.SMEM)] + [vmem] * 4,
        out_specs=[vmem, vmem, vmem],
        out_shape=[jax.ShapeDtypeStruct((members, rows, 128), bf16), piece, piece],
        scratch_shapes=[
            pltpu.VMEM((total, 128), bf16),
            pltpu.VMEM((128, total), bf16),
            pltpu.VMEM((MOST_DOC + BQ + BK, BQ), f32),
            pltpu.VMEM((MOST_DOC + BQ + BK, BQ), f32),
            pltpu.VMEM((total, 128), f32),
            pltpu.VMEM((32, BQ), f32),
        ],
        compiler_params=pltpu.CompilerParams(vmem_limit_bytes=VMEM_LIMIT),
        cost_estimate=pl.CostEstimate(
            flops=1_000_000_000_000, transcendentals=10_000_000, bytes_accessed=20_000_000
        ),
        name="attend",
    )(scal, lo, qd, kv, kv_other)


def join_kernel(own_ref, got_ref, out):
    lane = lax.broadcasted_iota(jnp.int32, own_ref.shape, 2)
    scale = jnp.where(lane < 64, HEAD_DIM ** (-0.5), 1.0)
    out[...] = ((own_ref[...] + got_ref[...]) * scale).astype(bf16)


def join(own, got):
    members, rows, _ = own.shape
    two = pl.BlockSpec((2, rows, 128), lambda m: (m, 0, 0))
    return pl.pallas_call(
        join_kernel,
        grid=(members // 2,),
        in_specs=[two] * 2,
        out_specs=two,
        out_shape=jax.ShapeDtypeStruct((members, rows, 128), bf16),
        name="join",
    )(own, got)


def side_by_side(x_ref, c_ref, s_ref, front_ref, back_ref):
    members, rows, _ = x_ref.shape
    lane = lax.broadcasted_iota(jnp.int32, (rows, 128), 1)
    low = lane < 64
    cos_tab = c_ref[...]
    sine_tab = -s_ref[...]
    for pair in range(members // 2):
        a = x_ref[2 * pair].astype(f32)
        b = x_ref[2 * pair + 1].astype(f32)
        cut = slice(128 * pair, 128 * pair + 128)
        front = jnp.where(low, a, pltpu.roll(b, 64, 1))
        front_ref[:, cut] = turn(front, cos_tab, sine_tab, lane).astype(bf16)
        back_ref[:, cut] = jnp.where(low, pltpu.roll(a, 64, 1), b).astype(bf16)


def query_grad_kernel(share, x_ref, c_ref, s_ref, h_ref, g_ref, dq_ref, att_ref, out):
    side_by_side(x_ref, c_ref, s_ref, dq_ref, att_ref)
    half = dq_ref.shape[1]
    out[:, :half] = mm(h_ref[...], dq_ref[...], ((0,), (0,))).astype(bf16)
    g_out = mm(att_ref[...], g_ref[...], ((0,), (0,))).astype(bf16)
    for i in range(half // share):
        rows = slice(i * share, (i + 1) * share)
        out[2 * i * share : (2 * i + 1) * share, half:] = g_out[rows, : D // 2]
        out[(2 * i + 1) * share : (2 * i + 2) * share, half:] = g_out[rows, D // 2 :]


def query_plain_kernel(x_ref, c_ref, s_ref, dq_ref, att_ref):
    side_by_side(x_ref, c_ref, s_ref, dq_ref, att_ref)


def query_grads(x, cos_tab, sine_tab, hidden, cotangent, share):
    members, rows, _ = x.shape
    half = members * HEAD_DIM
    vmem = pl.BlockSpec(memory_space=pltpu.VMEM)
    flat = jax.ShapeDtypeStruct((rows, half), bf16)
    params = pltpu.CompilerParams(vmem_limit_bytes=VMEM_LIMIT)
    if share % 32 == 0:
        return pl.pallas_call(
            functools.partial(query_grad_kernel, share),
            in_specs=[vmem] * 5,
            out_specs=[vmem] * 3,
            out_shape=[flat, flat, jax.ShapeDtypeStruct((D, D), bf16)],
            compiler_params=params,
            name="query_grads",
        )(x, cos_tab, sine_tab, hidden, cotangent)
    d_query, attended = pl.pallas_call(
        query_plain_kernel,
        in_specs=[vmem] * 3,
        out_specs=[vmem] * 2,
        out_shape=[flat, flat],
        compiler_params=params,
        name="query_plain",
    )(x, cos_tab, sine_tab)
    g_query = mm(hidden, d_query, ((0,), (0,))).astype(bf16)
    g_out = mm(attended, cotangent, ((0,), (0,))).astype(bf16)
    packed = g_out.reshape(half // share, share, 2, D // 2).transpose(0, 2, 1, 3)
    return d_query, attended, jnp.concatenate([g_query, packed.reshape(D, D // 2)], axis=1)


def key_grad_kernel(x_ref, c_ref, s_ref, h_ref, dkv_ref, out):
    half = dkv_ref.shape[1] // 2
    side_by_side(x_ref, c_ref, s_ref, dkv_ref.at[:, :half], dkv_ref.at[:, half:])
    out[...] = mm(h_ref[...], dkv_ref[...], ((0,), (0,))).astype(bf16)


def key_grads(x, cos_tab, sine_tab, hidden):
    members, rows, _ = x.shape
    vmem = pl.BlockSpec(memory_space=pltpu.VMEM)
    return pl.pallas_call(
        key_grad_kernel,
        in_specs=[vmem] * 4,
        out_specs=[vmem, vmem],
        out_shape=[
            jax.ShapeDtypeStruct((rows, 2 * members * HEAD_DIM), bf16),
            jax.ShapeDtypeStruct((D, D), bf16),
        ],
        compiler_params=pltpu.CompilerParams(vmem_limit_bytes=VMEM_LIMIT),
        name="key_grads",
    )(x, cos_tab, sine_tab, hidden)


def place_kernel(sel, near_one, far_one, near_two, far_two, near_a, far_a, near_b, far_b, out):
    step = pl.program_id(0)
    rows = out.shape[1]
    half = D // 2
    share = rows // 2

    def attn_slot(ones, twos):
        for top in range(2):
            for part in range(2):
                first = part * half
                one = ones[top]
                two = twos[top]
                out[top, :, first : first + half] = one[0, part, :, :half].astype(f32)
                first = first + D
                out[top, :, first : first + half] = two[0, part, :, :half].astype(f32)
                first = first + D
                out[top, :, first : first + half] = two[0, part, :, half:].astype(f32)

    def feed_slot(ones, twos):
        for top in range(2):
            for part in range(2):
                first = 2 * part * D
                out[top, :, first : first + D] = ones[top][0, part, :, :].astype(f32)
                first = first + D
                out[top, :, first : first + D] = twos[top][0, part, :, :].astype(f32)

    def last_columns(sources):
        for which, source in enumerate(sources):
            for part in range(2):
                for side in range(2):
                    first = 3 * D + side * half
                    picked = source[0, part, side * share : side * share + share, :]
                    to = slice(which * share, which * share + share)
                    out[part, to, first : first + half] = picked.astype(f32)

    for slot, fill in enumerate((attn_slot, feed_slot)):
        for own in range(2):
            @pl.when((sel[0] == slot) & (sel[1] == own))
            def _():
                if own == 0:
                    fill((near_one, far_one), (near_two, far_two))
                else:
                    fill((far_one, near_one), (far_two, near_two))

    use_near = (step < pl.num_programs(0) // 2) == (sel[1] == 0)

    @pl.when((sel[0] == 0) & use_near)
    def _():
        last_columns((near_a, near_b))

    @pl.when((sel[0] == 0) & jnp.logical_not(use_near))
    def _():
        last_columns((far_a, far_b))


def place_slot(near_one, far_one, near_two, far_two, sel):
    half = near_one.shape[0]
    rows = near_one.shape[2]
    shape = (1, 2, rows, D)

    def by_pair(offset):
        return pl.BlockSpec(shape, lambda i, sel: (i ^ sel[offset], 0, 0, 0))

    def out_spec(own, which):
        def index(i, sel):
            block = 2 * i + which
            used = (sel[0] == 0) & ((block < half) == (sel[1] == own))
            return (jnp.where(used, (block % half) ^ sel[2], half - 1), 0, 0, 1)

        return pl.BlockSpec((1, 2, rows, D // 2), index)

    placed = pl.pallas_call(
        place_kernel,
        grid_spec=pltpu.PrefetchScalarGridSpec(
            num_scalar_prefetch=1,
            grid=(half,),
            in_specs=[by_pair(2), by_pair(2), by_pair(3), by_pair(3)]
            + [out_spec(own, which) for which in range(2) for own in range(2)],
            out_specs=pl.BlockSpec((2, rows, FF), lambda i, sel: (0, i, 0)),
        ),
        out_shape=jax.ShapeDtypeStruct((2, D // 2, FF), f32),
        compiler_params=pltpu.CompilerParams(vmem_limit_bytes=VMEM_LIMIT),
        name="place",
    )(sel, near_one, far_one, near_two, far_two, near_one, far_one, near_one, far_one)
    return placed.reshape(D, FF)


def body(inputs, cotangent, doc_lengths, pad_counts, ln_gain, ln_bias,
         w_first, b_first, w_second, b_second):
    rows = inputs.shape[0]
    count = lax.axis_size("seq")
    span = SEQ_LEN // rows
    lead = span // 2
    members = span // 2
    half = members * HEAD_DIM
    half_ff = FF // 2
    seq_at = lax.axis_index("seq")
    branch = lax.axis_index("pair")
    on_first = branch == 0
    block_at = (seq_at - lead) % count
    seq_no = block_at // span
    block_in = block_at % span
    place = block_in // 2
    parity = block_in % 2

    def device_of(block):
        return (block + lead) % count

    def seq_swap(bit):
        return [(i, i ^ bit) for i in range(count)]

    core_swap = [(device_of(b), device_of(b ^ 1)) for b in range(count)]

    weights = w_first[0]
    ids = jnp.arange(rows, dtype=jnp.int32)

    widened = inputs.astype(f32)
    centred = widened - jnp.mean(widened, axis=1, keepdims=True)
    rstd = lax.rsqrt(jnp.mean(centred * centred, axis=1, keepdims=True) + epsilon)
    hidden = (centred * rstd * ln_gain + ln_bias).astype(bf16)

    core = parity
    half_d = D // 2
    to_second = [(2 * i, 2 * i + 1) for i in range(count)]
    to_first = [(2 * i + 1, 2 * i) for i in range(count)]
    both_ways = [(0, 1), (1, 0)]

    def my_rows(at, width):
        return lax.dynamic_slice(weights, (core * half_d, at), (half_d, width))

    def columns(slot_part, index):
        at = slot_part * D + index * half
        return weights[:, at : at + half]

    def both_cores(got):
        other = lax.ppermute(got, "seq", core_swap)
        return (jnp.where(core == 0, got, other), jnp.where(core == 0, other, got))

    out_second = lax.dynamic_slice(weights, (half, 3 * D + core * half_d), (half, half_d))
    kv_sent = jnp.concatenate([my_rows(j * D + half, half) for j in (1, 2)], axis=1)
    kv_crossed = lax.ppermute(kv_sent, ("seq", "pair"), to_second)
    qo_sent = after(jnp.concatenate([my_rows(half, half), out_second], axis=1), kv_crossed)
    qo_crossed = lax.ppermute(qo_sent, ("seq", "pair"), to_second)
    up_crossed = lax.ppermute(my_rows(0, half_ff), ("seq", "pair"), to_first)
    b_other = lax.ppermute(b_first, "pair", both_ways)
    own_blocks = 2 * jnp.arange(members, dtype=jnp.int32) + parity
    own_pos = (own_blocks[:, None] * rows + ids[None, :]).reshape(-1)
    cos_q, sine_q = rotation_tables(block_in * rows + ids, 64)
    kv_low, kv_high = both_cores(kv_crossed)
    w_kv = jnp.where(
        on_first,
        jnp.concatenate([columns(1, 0), columns(2, 0)], axis=1),
        jnp.concatenate([kv_low, kv_high], axis=0),
    )
    b_attn = jnp.where(on_first, b_first[0], b_other[0])
    b_q, b_k, b_v = (
        lax.dynamic_slice(b_attn, (j * D + branch * half,), (half,)) for j in range(3)
    )
    kv_heads = project(
        hidden, hidden, w_kv[:, :half], w_kv[:, half:], b_k, b_v, cos_q, sine_q, False
    )
    qo_low, qo_high = both_cores(after(qo_crossed, kv_heads))
    w_q = jnp.where(
        on_first, columns(0, 0), jnp.concatenate([qo_low[:, :half], qo_high[:, :half]], axis=0)
    )
    w_out = jnp.where(
        on_first,
        weights[:half, 3 * D :],
        jnp.concatenate([qo_low[:, half:], qo_high[:, half:]], axis=1),
    )

    groups = [
        [device_of(n * span + 2 * m + k) for m in range(members)]
        for n in range(count // span)
        for k in range(2)
    ]

    def spread(blocks):
        return lax.all_to_all(blocks, "seq", 0, 0, axis_index_groups=groups)

    kv_own = spread(kv_heads)
    kv_other = lax.ppermute(kv_own, "seq", core_swap)
    qd_heads = project(
        hidden, cotangent, w_q, w_out, b_q, jnp.zeros_like(b_q), cos_q, sine_q, True
    )
    qd_own = spread(qd_heads)

    bits = list(range(count.bit_length() - 1))
    path_one = list(bits)
    path_two = [bits[0], bits[2], bits[1]] + bits[3:]

    def in_path(index, path):
        moved = [((index >> b) & 1) << (len(path) - 1 - i) for i, b in enumerate(path)]
        return functools.reduce(lambda x, y: x | y, moved)

    up_low, up_high = both_cores(up_crossed)
    w_up = jnp.where(on_first, jnp.concatenate([up_low, up_high], axis=0), weights[:, half_ff:])
    w_up = after(w_up, kv_other, qd_heads)
    b_up = jnp.where(on_first, b_other[0, :half_ff], b_first[0, half_ff:])
    w_down = lax.dynamic_slice(w_second, (branch * half_ff, 0), (half_ff, D))
    root_half = 0.7071067811865476
    up_proj = mm(hidden, w_up, ((1,), (0,))) + b_up
    cdf = 0.5 * (1.0 + lax.erf(up_proj * root_half))
    active = (up_proj * cdf).astype(bf16)
    slope = cdf + up_proj * jnp.exp(up_proj * up_proj * -0.5) * 0.3989422804014327
    d_active = mm(cotangent, w_down, ((1,), (1,)))
    d_up = (d_active * slope).astype(bf16)
    orders = [[in_path(i, path) for i in range(count)] for path in (path_one, path_two)]
    g_feed = feed_grads(hidden, d_up, active, cotangent, orders)
    up_bias = jnp.sum(d_up, axis=0, dtype=f32)
    feed_shard = lax.psum_scatter(g_feed, "seq", scatter_dimension=0, tiled=True)[0]

    def scatter_step(array, b):
        size, cols = array.shape
        bit = (seq_at >> b) & 1
        split = array.reshape(2, size // 2, cols)
        keep = lax.dynamic_index_in_dim(split, bit, 0, keepdims=False)
        send = lax.dynamic_index_in_dim(split, 1 - bit, 0, keepdims=False)
        got = lax.ppermute(send, "seq", seq_swap(1 << b))
        return (keep.astype(f32) + got.astype(f32)).astype(bf16)

    def gather_step(array, b):
        return jnp.concatenate([array, lax.ppermute(array, "seq", seq_swap(1 << b))], axis=0)

    doc_row = lax.dynamic_index_in_dim(doc_lengths, seq_no, 0, keepdims=False)
    pads = lax.dynamic_index_in_dim(pad_counts, seq_no, 0, keepdims=False)
    bounds = jnp.cumsum(doc_row)
    start = jnp.max(jnp.where(bounds[:, None] <= own_pos[None, :], bounds[:, None], 0), axis=0)
    lo = jnp.where(own_pos >= SEQ_LEN - pads, own_pos, start)
    lo = lo.reshape(-1, BQ)
    scal = jnp.concatenate([parity[None], lo[:, 0]]).astype(jnp.int32)
    qd_own = after(qd_own, g_feed)
    dq_att, dkv_own, dkv_send = attend(scal, lo, qd_own, kv_own, kv_other)
    dkv_got = lax.ppermute(dkv_send, "seq", core_swap)
    active = after(active, dq_att)
    d_up = after(d_up, dq_att)
    feed_out = mm(active, w_down, ((1,), (0,)))
    d_hidden_feed = mm(d_up, w_up, ((1,), (1,)))
    dq_att = spread(dq_att)
    d_kv = join(dkv_own, dkv_got)
    dq_att, d_kv, feed_out, d_hidden_feed = lax.optimization_barrier(
        (dq_att, d_kv, feed_out, d_hidden_feed)
    )
    d_kv = spread(d_kv)

    share = half // count
    d_query, attended, g_one = query_grads(dq_att, cos_q, sine_q, hidden, cotangent, share)
    attn_one = scatter_step(scatter_step(g_one, path_one[0]), path_one[1])
    d_hidden = mm(d_query, w_q, ((1,), (1,))) + d_hidden_feed
    out_part = mm(attended, w_out, ((1,), (0,))) + feed_out
    out_low = (out_part + jnp.where(on_first, b_first[0, 3 * D :], 0.0)).astype(bf16)
    d_kv, feed_shard, attn_one, d_hidden, out_low = lax.optimization_barrier(
        (d_kv, feed_shard, attn_one, d_hidden, out_low)
    )
    down_all = lax.all_gather(feed_shard[2:], "seq", axis=1, tiled=True)

    d_keys, g_two = key_grads(d_kv, cos_q, sine_q, hidden)
    d_hidden = d_hidden + mm(d_keys, w_kv, ((1,), (1,)))
    d_hidden_low = d_hidden.astype(bf16)

    def in_half(vector):
        zero = jnp.zeros_like(vector)
        return jnp.stack([jnp.where(on_first, vector, zero), jnp.where(on_first, zero, vector)])

    normal = centred * rstd
    q_bias = jnp.sum(d_query, axis=0, dtype=f32)
    kv_bias = jnp.sum(d_keys, axis=0, dtype=f32)
    qkv_bias = jnp.concatenate([q_bias, kv_bias]).reshape(3, half)
    cot_sum = jnp.where(on_first, jnp.sum(cotangent, axis=0, dtype=f32), 0.0)
    small = jnp.concatenate(
        [
            in_half(qkv_bias).transpose(1, 0, 2).reshape(-1),
            in_half(up_bias).reshape(-1),
            cot_sum,
            jnp.sum(d_hidden * normal, axis=0),
            jnp.sum(d_hidden, axis=0),
        ]
    ).reshape(-1, 128)

    attn_two = g_two
    out_other = lax.ppermute(out_low, "pair", both_ways)
    ahead = list(path_one[2:])
    for i, b in enumerate(path_two):
        if ahead:
            attn_one = scatter_step(attn_one, ahead.pop(0))
        attn_two = scatter_step(attn_two, b)
        attn_one, attn_two = lax.optimization_barrier((attn_one, attn_two))
        if i == len(path_two) - 1:
            attn_one, attn_two, down_all = lax.optimization_barrier(
                (attn_one, attn_two, down_all)
            )
        if i == 1:
            attn_two, d_hidden_low, small = lax.optimization_barrier(
                (attn_two, d_hidden_low, small)
            )
        if i == 2:
            attn_two, out_other = lax.optimization_barrier((attn_two, out_other))

    attn_both = jnp.stack([attn_one, attn_two])
    feed_both = feed_shard[:2]
    other = lax.ppermute(jnp.where(on_first, feed_both, attn_both), "pair", both_ways)
    zero_slot = jnp.where(on_first, attn_both, other)
    one_slot = jnp.where(on_first, other, feed_both)
    near_one = jnp.stack([zero_slot[0], one_slot[0]])[None]
    near_two = jnp.stack([zero_slot[1], one_slot[1]])[None]
    crossed = after(d_hidden_low, near_one, near_two)
    crossed = lax.ppermute(crossed, "pair", both_ways)
    small = small + lax.ppermute(small, "pair", both_ways)
    for i in range(len(bits) - 1, 0, -1):
        near_one = gather_step(near_one, path_one[i])
        near_two = gather_step(near_two, path_two[i])
        small = small + lax.ppermute(small, "seq", seq_swap(1 << path_two[i]))
        near_one, near_two, small = lax.optimization_barrier((near_one, near_two, small))
        if i == 2:
            crossed, down_all = lax.optimization_barrier((crossed, down_all, near_two))[:2]
    outputs = (widened + b_second + (out_low.astype(f32) + out_other.astype(f32))).astype(bf16)
    e = (d_hidden_low.astype(f32) + crossed.astype(f32)) * ln_gain
    d_norm = rstd * (
        e
        - jnp.mean(e, axis=1, keepdims=True)
        - normal * jnp.mean(e * normal, axis=1, keepdims=True)
    )
    d_inputs = (cotangent.astype(f32) + d_norm).astype(bf16)

    my_one = in_path(seq_at, path_one)
    my_two = in_path(seq_at, path_two)
    d_w_second = down_all.reshape(half_ff, D).astype(f32)
    near_two, outputs, d_inputs, d_w_second = lax.optimization_barrier(
        (near_two, outputs, d_inputs, d_w_second)
    )
    far_two = lax.ppermute(near_two, "seq", seq_swap(1 << path_two[0]))
    small = small + lax.ppermute(small, "seq", seq_swap(1 << path_two[0]))
    far_one = lax.ppermute(near_one, "seq", seq_swap(1 << path_one[0]))
    small = small.reshape(-1)
    if share % 32 == 0:
        low_bits = count // 2 - 1
        sel = jnp.stack([branch, core, my_one & low_bits, my_two & low_bits]).astype(jnp.int32)
        d_w_first = place_slot(near_one, far_one, near_two, far_two, sel)
    else:
        order = jnp.arange(count, dtype=jnp.int32)
        full_one = jnp.take(jnp.concatenate([near_one, far_one]), order ^ my_one, axis=0)
        full_two = jnp.take(jnp.concatenate([near_two, far_two]), order ^ my_two, axis=0)
        full_one = full_one.transpose(1, 0, 2, 3).reshape(2, D, D)
        full_two = full_two.transpose(1, 0, 2, 3).reshape(2, D, D)
        unpacked = full_one[:, :, half:].reshape(2, count, 2, share, half)
        unpacked = unpacked.transpose(0, 1, 3, 2, 4).reshape(D, D)
        as_attn = jnp.concatenate(
            [
                full_one[0, :, :half], full_one[1, :, :half],
                full_two[0, :, :half], full_two[1, :, :half],
                full_two[0, :, half:], full_two[1, :, half:],
                unpacked,
            ],
            axis=1,
        )
        as_feed = jnp.concatenate([full_one[0], full_two[0], full_one[1], full_two[1]], axis=1)
        d_w_first = jnp.where(on_first, as_attn, as_feed).astype(f32)

    cot_total = small[3 * D + FF : 4 * D + FF]
    d_b_first = jnp.where(
        on_first, jnp.concatenate([small[: 3 * D], cot_total]), small[3 * D : 3 * D + FF]
    )
    return (
        outputs,
        d_inputs,
        small[4 * D + FF : 5 * D + FF],
        small[5 * D + FF :],
        d_w_first[None],
        d_b_first[None],
        d_w_second,
        cot_total,
    )


def solution(mesh):
    in_specs = (
        P("seq", None),
        P("seq", None),
        P(),
        P(),
        P(),
        P(),
        P("pair", None, None),
        P("pair", None),
        P(),
        P(),
    )
    out_specs = (
        P("seq", None),
        P("seq", None),
        P(),
        P(),
        P("pair", None, None),
        P("pair", None),
        P("pair", None),
        P(),
    )
    return jax.shard_map(body, mesh=mesh, in_specs=in_specs, out_specs=out_specs, check_vma=False)
```

```python
import functools

import jax
import jax.numpy as jnp
from jax import lax
from jax.experimental import pallas as pl
from jax.experimental.pallas import tpu as pltpu
from jax.sharding import PartitionSpec as P

HEADS = 16
HEAD_DIM = 64
D = 1024
FF = 4096
ROT = 16
SEQ_LEN = 8192
DOCS = 8
MOST_DOC = 4096

BQ = 512
BK = 512
epsilon = 1e-05
masked_fill = -1e30
bf16 = jnp.bfloat16
f32 = jnp.float32
VMEM_LIMIT = 60 * 1024 * 1024


def after(array, *others):
    return lax.optimization_barrier((array,) + others)[0]


def mm(left, right, dims):
    return lax.dot_general(left, right, (dims, ((), ())), preferred_element_type=f32)


def rotation_tables(positions, period):
    lane = lax.broadcasted_iota(jnp.int32, (positions.shape[0], 128), 1) % period
    inverse = 10000.0 ** (-2.0 * (lane % (ROT // 2)).astype(f32) / ROT)
    angle = positions.astype(f32)[:, None] * inverse
    cos_tab = jnp.where(lane < ROT, jnp.cos(angle), 1.0)
    sine = jnp.sin(angle)
    sine_tab = jnp.where(lane < ROT // 2, -sine, jnp.where(lane < ROT, sine, 0.0))
    return cos_tab, sine_tab


def turn(block, cos_tab, sine_tab, lane):
    from_left = pltpu.roll(block, 8, 1)
    from_right = pltpu.roll(block, 120, 1)
    return block * cos_tab + jnp.where(lane % 64 < 8, from_right, from_left) * sine_tab


def project_kernel(turned, x_ref, y_ref, wx, wy, bx, by, c_ref, s_ref, out):
    rows = x_ref.shape[0]
    lane = lax.broadcasted_iota(jnp.int32, (rows, 128), 1)
    low = lane < 64
    front_all = mm(x_ref[...], wx[...], ((1,), (0,))) + bx[...]
    back_all = mm(y_ref[...], wy[...], ((1,), (1 if turned else 0,))) + by[...]
    cos_tab = c_ref[...]
    sine_tab = s_ref[...]
    for pair in range(wx.shape[1] // 128):
        cut = slice(128 * pair, 128 * pair + 128)
        front = turn(front_all[:, cut], cos_tab, sine_tab, lane)
        back = back_all[:, cut]
        out[2 * pair] = jnp.where(low, front, pltpu.roll(back, 64, 1)).astype(bf16)
        out[2 * pair + 1] = jnp.where(low, pltpu.roll(front, 64, 1), back).astype(bf16)


def project(left, right, w_left, w_right, b_left, b_right, cos_tab, sine_tab, turned):
    rows = left.shape[0]
    heads = w_left.shape[1] // HEAD_DIM
    whole = lambda i: (0, 0)
    part = lambda i: (0, i)
    if turned:
        right_spec = pl.BlockSpec((256, D), lambda i: (i, 0))
    else:
        right_spec = pl.BlockSpec((D, 256), part)
    return pl.pallas_call(
        functools.partial(project_kernel, turned),
        grid=(heads // 4,),
        in_specs=[
            pl.BlockSpec((rows, D), whole),
            pl.BlockSpec((rows, D), whole),
            pl.BlockSpec((D, 256), part),
            right_spec,
            pl.BlockSpec((1, 256), part),
            pl.BlockSpec((1, 256), part),
            pl.BlockSpec((rows, 128), whole),
            pl.BlockSpec((rows, 128), whole),
        ],
        out_specs=pl.BlockSpec((4, rows, 128), lambda i: (i, 0, 0)),
        out_shape=jax.ShapeDtypeStruct((heads, rows, 128), bf16),
        compiler_params=pltpu.CompilerParams(vmem_limit_bytes=VMEM_LIMIT),
        name="project_q" if turned else "project_kv",
    )(left, right, w_left, w_right, b_left[None], b_right[None], cos_tab, sine_tab)


def feed_grad_kernel(orders, h_ref, u_ref, a_ref, g_ref, out):
    step = pl.program_id(0)
    size = out.shape[2]

    for part in range(4):
        @pl.when(step == part)
        def _():
            left, right = (h_ref, u_ref) if part < 2 else (a_ref, g_ref)
            total = mm(left[...], right[...], ((0,), (0,))).astype(bf16)
            order = orders[part] if part < 2 else range(out.shape[0])
            for i, block in enumerate(order):
                out[i, 0] = total[block * size : block * size + size]


def feed_grads(hidden, d_up, active, cotangent, orders):
    rows = hidden.shape[0]
    count = len(orders[0])
    whole = lambda i: (0, 0)
    return pl.pallas_call(
        functools.partial(feed_grad_kernel, orders),
        grid=(4,),
        in_specs=[
            pl.BlockSpec((rows, D), whole),
            pl.BlockSpec((rows, D), lambda i: (0, jnp.minimum(i, 1))),
            pl.BlockSpec((rows, D), lambda i: (0, jnp.maximum(i - 2, 0))),
            pl.BlockSpec((rows, D), whole),
        ],
        out_specs=pl.BlockSpec((count, 1, D // count, D), lambda i: (0, i, 0, 0)),
        out_shape=jax.ShapeDtypeStruct((count, 4, D // count, D), bf16),
        compiler_params=pltpu.CompilerParams(vmem_limit_bytes=VMEM_LIMIT),
        name="feed_grads",
    )(hidden, d_up, active, cotangent)


def attend_kernel(scal, lo_ref, qd_ref, kv_ref, kvp_ref, dq_ref, own_ref, send_ref,
                  kv_s, kvt_s, s_buf, p_buf, acc_s, m_s):
    members, rows, _ = qd_ref.shape
    parity = scal[0]
    scale = HEAD_DIM ** (-0.5)
    to_two = scale * 1.4426950408889634

    for m in range(members):
        at_own = pl.multiple_of((2 * m + parity) * rows, rows)
        at_other = pl.multiple_of((2 * m + 1 - parity) * rows, rows)
        kv_s[pl.ds(at_own, rows), :] = kv_ref[m]
        kv_s[pl.ds(at_other, rows), :] = kvp_ref[m]
    acc_s[...] = jnp.zeros_like(acc_s)

    def transpose_step(b, carry):
        at = pl.multiple_of(b * 256, 256)
        kvt_s[:, pl.ds(at, 256)] = kv_s[pl.ds(at, 256), :].astype(f32).T.astype(bf16)
        return carry

    lax.fori_loop(0, kv_s.shape[0] // 256, transpose_step, 0)

    per = rows // BQ
    lane = lax.broadcasted_iota(jnp.int32, (BQ, 128), 1)
    key_iota = lax.broadcasted_iota(jnp.int32, (BK, BQ), 0)
    query_iota = lax.broadcasted_iota(jnp.int32, (1, BQ), 1)

    def query_block(i, carry):
        m = i // per
        part = i % per
        off = pl.multiple_of(part * BQ, BQ)
        first = (2 * m + parity) * rows + off
        qd = qd_ref[m, pl.ds(off, BQ), :]
        zero = jnp.zeros_like(qd)
        qz = jnp.where(lane < 64, qd, zero)
        dz = jnp.where(lane < 64, zero, qd)
        both = jnp.concatenate([qz, dz], axis=0)
        kb0 = scal[1 + i] // BK
        kb1 = (first + BQ - 1) // BK + 1
        qpos = first + query_iota
        lo = lo_ref[pl.ds(i, 1), :]

        def scores_step(kb, sums):
            top, total, dots = sums
            at = pl.multiple_of(kb * BK, BK)
            r = mm(kv_s[pl.ds(at, BK), :], both, ((1,), (1,)))
            kpos = at + key_iota
            s = jnp.where((kpos <= qpos) & (kpos >= lo), r[:, :BQ], masked_fill)
            eights = jnp.max(s.reshape(BK // 8, 8, BQ), axis=0)
            new_top = jnp.maximum(top, jnp.max(eights, axis=0, keepdims=True))
            e = jnp.exp2((s - new_top) * to_two)
            w = e * r[:, BQ:]
            to = pl.multiple_of((kb - kb0) * BK, BK)
            s_buf[pl.ds(to, BK), :] = e
            p_buf[pl.ds(to, BK), :] = r[:, BQ:]
            m_s[pl.ds(kb - kb0, 1), :] = new_top
            shrink = jnp.exp2((top - new_top) * to_two)
            return (new_top,
                    total * shrink + jnp.sum(e.reshape(BK // 8, 8, BQ), axis=0),
                    dots * shrink + jnp.sum(w.reshape(BK // 8, 8, BQ), axis=0))

        zeros = jnp.zeros((8, BQ), f32)
        lowest = jnp.full((1, BQ), masked_fill, f32)
        top, total, dots = lax.fori_loop(kb0, kb1, scores_step, (lowest, zeros, zeros))
        inv = 1.0 / jnp.sum(total, axis=0, keepdims=True)
        row_dot = jnp.sum(dots, axis=0, keepdims=True) * inv

        def grad_step(kb, outs):
            dq_t, at_t = outs
            at = pl.multiple_of(kb * BK, BK)
            to = pl.multiple_of((kb - kb0) * BK, BK)
            share = jnp.exp2((m_s[pl.ds(kb - kb0, 1), :] - top) * to_two) * inv
            p = s_buf[pl.ds(to, BK), :] * share
            ds = p * (p_buf[pl.ds(to, BK), :] - row_dot)
            p_low = p.astype(bf16)
            ds_low = ds.astype(bf16)
            joined = jnp.concatenate([ds_low, p_low], axis=1)
            acc_s[pl.ds(at, BK), :] += mm(joined, both, ((1,), (0,)))
            dq_t = dq_t + mm(kvt_s[0:64, pl.ds(at, BK)], ds_low, ((1,), (0,)))
            at_t = at_t + mm(kvt_s[64:128, pl.ds(at, BK)], p_low, ((1,), (0,)))
            return dq_t, at_t

        wide = jnp.zeros((64, BQ), f32)
        dq_t, at_t = lax.fori_loop(kb0, kb1, grad_step, (wide, wide))
        done = jnp.concatenate([dq_t * scale, at_t], axis=0).T
        dq_ref[m, pl.ds(off, BQ), :] = done.astype(bf16)
        return carry

    lax.fori_loop(0, members * per, query_block, 0)

    for m in range(members):
        at_own = pl.multiple_of((2 * m + parity) * rows, rows)
        at_other = pl.multiple_of((2 * m + 1 - parity) * rows, rows)
        own_ref[m] = acc_s[pl.ds(at_own, rows), :]
        send_ref[m] = acc_s[pl.ds(at_other, rows), :]


def attend(scal, lo, qd, kv, kv_other):
    members, rows, _ = qd.shape
    total = 2 * members * rows
    piece = jax.ShapeDtypeStruct((members, rows, 128), f32)
    vmem = pl.BlockSpec(memory_space=pltpu.VMEM)
    return pl.pallas_call(
        attend_kernel,
        in_specs=[pl.BlockSpec(memory_space=pltpu.SMEM)] + [vmem] * 4,
        out_specs=[vmem, vmem, vmem],
        out_shape=[jax.ShapeDtypeStruct((members, rows, 128), bf16), piece, piece],
        scratch_shapes=[
            pltpu.VMEM((total, 128), bf16),
            pltpu.VMEM((128, total), bf16),
            pltpu.VMEM((MOST_DOC + BQ + BK, BQ), f32),
            pltpu.VMEM((MOST_DOC + BQ + BK, BQ), f32),
            pltpu.VMEM((total, 128), f32),
            pltpu.VMEM((32, BQ), f32),
        ],
        compiler_params=pltpu.CompilerParams(vmem_limit_bytes=VMEM_LIMIT),
        cost_estimate=pl.CostEstimate(
            flops=1_000_000_000_000, transcendentals=10_000_000, bytes_accessed=20_000_000
        ),
        name="attend",
    )(scal, lo, qd, kv, kv_other)


def join_kernel(own_ref, got_ref, out):
    lane = lax.broadcasted_iota(jnp.int32, own_ref.shape, 2)
    scale = jnp.where(lane < 64, HEAD_DIM ** (-0.5), 1.0)
    out[...] = ((own_ref[...] + got_ref[...]) * scale).astype(bf16)


def join(own, got):
    members, rows, _ = own.shape
    two = pl.BlockSpec((2, rows, 128), lambda m: (m, 0, 0))
    return pl.pallas_call(
        join_kernel,
        grid=(members // 2,),
        in_specs=[two] * 2,
        out_specs=two,
        out_shape=jax.ShapeDtypeStruct((members, rows, 128), bf16),
        name="join",
    )(own, got)


def side_by_side(x_ref, c_ref, s_ref, front_ref, back_ref):
    members, rows, _ = x_ref.shape
    lane = lax.broadcasted_iota(jnp.int32, (rows, 128), 1)
    low = lane < 64
    cos_tab = c_ref[...]
    sine_tab = -s_ref[...]
    for pair in range(members // 2):
        a = x_ref[2 * pair].astype(f32)
        b = x_ref[2 * pair + 1].astype(f32)
        cut = slice(128 * pair, 128 * pair + 128)
        front = jnp.where(low, a, pltpu.roll(b, 64, 1))
        front_ref[:, cut] = turn(front, cos_tab, sine_tab, lane).astype(bf16)
        back_ref[:, cut] = jnp.where(low, pltpu.roll(a, 64, 1), b).astype(bf16)


def query_grad_kernel(share, x_ref, c_ref, s_ref, h_ref, g_ref, dq_ref, att_ref, out):
    side_by_side(x_ref, c_ref, s_ref, dq_ref, att_ref)
    half = dq_ref.shape[1]
    out[:, :half] = mm(h_ref[...], dq_ref[...], ((0,), (0,))).astype(bf16)
    g_out = mm(att_ref[...], g_ref[...], ((0,), (0,))).astype(bf16)
    for i in range(half // share):
        rows = slice(i * share, (i + 1) * share)
        out[2 * i * share : (2 * i + 1) * share, half:] = g_out[rows, : D // 2]
        out[(2 * i + 1) * share : (2 * i + 2) * share, half:] = g_out[rows, D // 2 :]


def query_plain_kernel(x_ref, c_ref, s_ref, dq_ref, att_ref):
    side_by_side(x_ref, c_ref, s_ref, dq_ref, att_ref)


def query_grads(x, cos_tab, sine_tab, hidden, cotangent, share):
    members, rows, _ = x.shape
    half = members * HEAD_DIM
    vmem = pl.BlockSpec(memory_space=pltpu.VMEM)
    flat = jax.ShapeDtypeStruct((rows, half), bf16)
    params = pltpu.CompilerParams(vmem_limit_bytes=VMEM_LIMIT)
    if share % 32 == 0:
        return pl.pallas_call(
            functools.partial(query_grad_kernel, share),
            in_specs=[vmem] * 5,
            out_specs=[vmem] * 3,
            out_shape=[flat, flat, jax.ShapeDtypeStruct((D, D), bf16)],
            compiler_params=params,
            name="query_grads",
        )(x, cos_tab, sine_tab, hidden, cotangent)
    d_query, attended = pl.pallas_call(
        query_plain_kernel,
        in_specs=[vmem] * 3,
        out_specs=[vmem] * 2,
        out_shape=[flat, flat],
        compiler_params=params,
        name="query_plain",
    )(x, cos_tab, sine_tab)
    g_query = mm(hidden, d_query, ((0,), (0,))).astype(bf16)
    g_out = mm(attended, cotangent, ((0,), (0,))).astype(bf16)
    packed = g_out.reshape(half // share, share, 2, D // 2).transpose(0, 2, 1, 3)
    return d_query, attended, jnp.concatenate([g_query, packed.reshape(D, D // 2)], axis=1)


def key_grad_kernel(x_ref, c_ref, s_ref, h_ref, dkv_ref, out):
    half = dkv_ref.shape[1] // 2
    side_by_side(x_ref, c_ref, s_ref, dkv_ref.at[:, :half], dkv_ref.at[:, half:])
    out[...] = mm(h_ref[...], dkv_ref[...], ((0,), (0,))).astype(bf16)


def key_grads(x, cos_tab, sine_tab, hidden):
    members, rows, _ = x.shape
    vmem = pl.BlockSpec(memory_space=pltpu.VMEM)
    return pl.pallas_call(
        key_grad_kernel,
        in_specs=[vmem] * 4,
        out_specs=[vmem, vmem],
        out_shape=[
            jax.ShapeDtypeStruct((rows, 2 * members * HEAD_DIM), bf16),
            jax.ShapeDtypeStruct((D, D), bf16),
        ],
        compiler_params=pltpu.CompilerParams(vmem_limit_bytes=VMEM_LIMIT),
        name="key_grads",
    )(x, cos_tab, sine_tab, hidden)


def place_kernel(sel, near_one, far_one, near_two, far_two, near_a, far_a, near_b, far_b, out):
    step = pl.program_id(0)
    rows = out.shape[1]
    half = D // 2
    share = rows // 2

    def attn_slot(ones, twos):
        for top in range(2):
            for part in range(2):
                first = part * half
                one = ones[top]
                two = twos[top]
                out[top, :, first : first + half] = one[0, part, :, :half].astype(f32)
                first = first + D
                out[top, :, first : first + half] = two[0, part, :, :half].astype(f32)
                first = first + D
                out[top, :, first : first + half] = two[0, part, :, half:].astype(f32)

    def feed_slot(ones, twos):
        for top in range(2):
            for part in range(2):
                first = 2 * part * D
                out[top, :, first : first + D] = ones[top][0, part, :, :].astype(f32)
                first = first + D
                out[top, :, first : first + D] = twos[top][0, part, :, :].astype(f32)

    def last_columns(sources):
        for which, source in enumerate(sources):
            for part in range(2):
                for side in range(2):
                    first = 3 * D + side * half
                    picked = source[0, part, side * share : side * share + share, :]
                    to = slice(which * share, which * share + share)
                    out[part, to, first : first + half] = picked.astype(f32)

    for slot, fill in enumerate((attn_slot, feed_slot)):
        for own in range(2):
            @pl.when((sel[0] == slot) & (sel[1] == own))
            def _():
                if own == 0:
                    fill((near_one, far_one), (near_two, far_two))
                else:
                    fill((far_one, near_one), (far_two, near_two))

    use_near = (step < pl.num_programs(0) // 2) == (sel[1] == 0)

    @pl.when((sel[0] == 0) & use_near)
    def _():
        last_columns((near_a, near_b))

    @pl.when((sel[0] == 0) & jnp.logical_not(use_near))
    def _():
        last_columns((far_a, far_b))


def place_slot(near_one, far_one, near_two, far_two, sel):
    half = near_one.shape[0]
    rows = near_one.shape[2]
    shape = (1, 2, rows, D)

    def by_pair(offset):
        return pl.BlockSpec(shape, lambda i, sel: (i ^ sel[offset], 0, 0, 0))

    def out_spec(own, which):
        def index(i, sel):
            block = 2 * i + which
            used = (sel[0] == 0) & ((block < half) == (sel[1] == own))
            return (jnp.where(used, (block % half) ^ sel[2], half - 1), 0, 0, 1)

        return pl.BlockSpec((1, 2, rows, D // 2), index)

    placed = pl.pallas_call(
        place_kernel,
        grid_spec=pltpu.PrefetchScalarGridSpec(
            num_scalar_prefetch=1,
            grid=(half,),
            in_specs=[by_pair(2), by_pair(2), by_pair(3), by_pair(3)]
            + [out_spec(own, which) for which in range(2) for own in range(2)],
            out_specs=pl.BlockSpec((2, rows, FF), lambda i, sel: (0, i, 0)),
        ),
        out_shape=jax.ShapeDtypeStruct((2, D // 2, FF), f32),
        compiler_params=pltpu.CompilerParams(vmem_limit_bytes=VMEM_LIMIT),
        name="place",
    )(sel, near_one, far_one, near_two, far_two, near_one, far_one, near_one, far_one)
    return placed.reshape(D, FF)


def body(inputs, cotangent, doc_lengths, pad_counts, ln_gain, ln_bias,
         w_first, b_first, w_second, b_second):
    rows = inputs.shape[0]
    count = lax.axis_size("seq")
    span = SEQ_LEN // rows
    lead = span // 2
    members = span // 2
    half = members * HEAD_DIM
    half_ff = FF // 2
    seq_at = lax.axis_index("seq")
    branch = lax.axis_index("pair")
    on_first = branch == 0
    block_at = (seq_at - lead) % count
    seq_no = block_at // span
    block_in = block_at % span
    place = block_in // 2
    parity = block_in % 2

    def device_of(block):
        return (block + lead) % count

    def seq_swap(bit):
        return [(i, i ^ bit) for i in range(count)]

    core_swap = [(device_of(b), device_of(b ^ 1)) for b in range(count)]

    weights = w_first[0]
    ids = jnp.arange(rows, dtype=jnp.int32)

    widened = inputs.astype(f32)
    centred = widened - jnp.mean(widened, axis=1, keepdims=True)
    rstd = lax.rsqrt(jnp.mean(centred * centred, axis=1, keepdims=True) + epsilon)
    hidden = (centred * rstd * ln_gain + ln_bias).astype(bf16)

    core = parity
    half_d = D // 2
    to_second = [(2 * i, 2 * i + 1) for i in range(count)]
    to_first = [(2 * i + 1, 2 * i) for i in range(count)]
    both_ways = [(0, 1), (1, 0)]

    def my_rows(at, width):
        return lax.dynamic_slice(weights, (core * half_d, at), (half_d, width))

    def columns(slot_part, index):
        at = slot_part * D + index * half
        return weights[:, at : at + half]

    def both_cores(got):
        other = lax.ppermute(got, "seq", core_swap)
        return (jnp.where(core == 0, got, other), jnp.where(core == 0, other, got))

    out_second = lax.dynamic_slice(weights, (half, 3 * D + core * half_d), (half, half_d))
    kv_sent = jnp.concatenate([my_rows(j * D + half, half) for j in (1, 2)], axis=1)
    kv_crossed = lax.ppermute(kv_sent, ("seq", "pair"), to_second)
    qo_sent = after(jnp.concatenate([my_rows(half, half), out_second], axis=1), kv_crossed)
    qo_crossed = lax.ppermute(qo_sent, ("seq", "pair"), to_second)
    up_crossed = lax.ppermute(my_rows(0, half_ff), ("seq", "pair"), to_first)
    b_other = lax.ppermute(b_first, "pair", both_ways)
    own_blocks = 2 * jnp.arange(members, dtype=jnp.int32) + parity
    own_pos = (own_blocks[:, None] * rows + ids[None, :]).reshape(-1)
    cos_q, sine_q = rotation_tables(block_in * rows + ids, 64)
    kv_low, kv_high = both_cores(kv_crossed)
    w_kv = jnp.where(
        on_first,
        jnp.concatenate([columns(1, 0), columns(2, 0)], axis=1),
        jnp.concatenate([kv_low, kv_high], axis=0),
    )
    b_attn = jnp.where(on_first, b_first[0], b_other[0])
    b_q, b_k, b_v = (
        lax.dynamic_slice(b_attn, (j * D + branch * half,), (half,)) for j in range(3)
    )
    kv_heads = project(
        hidden, hidden, w_kv[:, :half], w_kv[:, half:], b_k, b_v, cos_q, sine_q, False
    )
    qo_low, qo_high = both_cores(after(qo_crossed, kv_heads))
    w_q = jnp.where(
        on_first, columns(0, 0), jnp.concatenate([qo_low[:, :half], qo_high[:, :half]], axis=0)
    )
    w_out = jnp.where(
        on_first,
        weights[:half, 3 * D :],
        jnp.concatenate([qo_low[:, half:], qo_high[:, half:]], axis=1),
    )

    groups = [
        [device_of(n * span + 2 * m + k) for m in range(members)]
        for n in range(count // span)
        for k in range(2)
    ]

    def spread(blocks):
        return lax.all_to_all(blocks, "seq", 0, 0, axis_index_groups=groups)

    kv_own = spread(kv_heads)
    w_down = lax.dynamic_slice(w_second, (branch * half_ff, 0), (half_ff, D))
    d_active = mm(cotangent, w_down, ((1,), (1,)))
    kv_own, d_active = lax.optimization_barrier((kv_own, d_active))
    kv_other = lax.ppermute(kv_own, "seq", core_swap)
    qd_heads = project(
        hidden, cotangent, w_q, w_out, b_q, jnp.zeros_like(b_q), cos_q, sine_q, True
    )
    qd_own = spread(qd_heads)

    bits = list(range(count.bit_length() - 1))
    path_one = list(bits)
    path_two = [bits[0], bits[2], bits[1]] + bits[3:]

    def in_path(index, path):
        moved = [((index >> b) & 1) << (len(path) - 1 - i) for i, b in enumerate(path)]
        return functools.reduce(lambda x, y: x | y, moved)

    up_low, up_high = both_cores(up_crossed)
    w_up = jnp.where(on_first, jnp.concatenate([up_low, up_high], axis=0), weights[:, half_ff:])
    w_up = after(w_up, kv_other, qd_heads)
    b_up = jnp.where(on_first, b_other[0, :half_ff], b_first[0, half_ff:])
    root_half = 0.7071067811865476
    up_proj = mm(hidden, w_up, ((1,), (0,))) + b_up
    cdf = 0.5 * (1.0 + lax.erf(up_proj * root_half))
    active = (up_proj * cdf).astype(bf16)
    slope = cdf + up_proj * jnp.exp(up_proj * up_proj * -0.5) * 0.3989422804014327
    d_up = (d_active * slope).astype(bf16)
    orders = [[in_path(i, path) for i in range(count)] for path in (path_one, path_two)]
    g_feed = feed_grads(hidden, d_up, active, cotangent, orders)
    up_bias = jnp.sum(d_up, axis=0, dtype=f32)
    feed_shard = lax.psum_scatter(g_feed, "seq", scatter_dimension=0, tiled=True)[0]

    def scatter_step(array, b):
        size, cols = array.shape
        bit = (seq_at >> b) & 1
        split = array.reshape(2, size // 2, cols)
        keep = lax.dynamic_index_in_dim(split, bit, 0, keepdims=False)
        send = lax.dynamic_index_in_dim(split, 1 - bit, 0, keepdims=False)
        got = lax.ppermute(send, "seq", seq_swap(1 << b))
        return (keep.astype(f32) + got.astype(f32)).astype(bf16)

    def gather_step(array, b):
        return jnp.concatenate([array, lax.ppermute(array, "seq", seq_swap(1 << b))], axis=0)

    doc_row = lax.dynamic_index_in_dim(doc_lengths, seq_no, 0, keepdims=False)
    pads = lax.dynamic_index_in_dim(pad_counts, seq_no, 0, keepdims=False)
    bounds = jnp.cumsum(doc_row)
    start = jnp.max(jnp.where(bounds[:, None] <= own_pos[None, :], bounds[:, None], 0), axis=0)
    lo = jnp.where(own_pos >= SEQ_LEN - pads, own_pos, start)
    lo = lo.reshape(-1, BQ)
    scal = jnp.concatenate([parity[None], lo[:, 0]]).astype(jnp.int32)
    qd_own = after(qd_own, g_feed)
    dq_att, dkv_own, dkv_send = attend(scal, lo, qd_own, kv_own, kv_other)
    dkv_got = lax.ppermute(dkv_send, "seq", core_swap)
    active = after(active, dq_att)
    d_up = after(d_up, dq_att)
    feed_out = mm(active, w_down, ((1,), (0,)))
    d_hidden_feed = mm(d_up, w_up, ((1,), (1,)))
    dq_att = spread(dq_att)
    d_kv = join(dkv_own, dkv_got)
    dq_att, d_kv, feed_out, d_hidden_feed = lax.optimization_barrier(
        (dq_att, d_kv, feed_out, d_hidden_feed)
    )
    d_kv = spread(d_kv)

    share = half // count
    d_query, attended, g_one = query_grads(dq_att, cos_q, sine_q, hidden, cotangent, share)
    attn_one = scatter_step(scatter_step(g_one, path_one[0]), path_one[1])
    d_hidden = mm(d_query, w_q, ((1,), (1,))) + d_hidden_feed
    out_part = mm(attended, w_out, ((1,), (0,))) + feed_out
    out_low = (out_part + jnp.where(on_first, b_first[0, 3 * D :], 0.0)).astype(bf16)
    d_kv, feed_shard, attn_one, d_hidden, out_low = lax.optimization_barrier(
        (d_kv, feed_shard, attn_one, d_hidden, out_low)
    )
    down_all = lax.all_gather(feed_shard[2:], "seq", axis=1, tiled=True)

    d_keys, g_two = key_grads(d_kv, cos_q, sine_q, hidden)
    d_hidden = d_hidden + mm(d_keys, w_kv, ((1,), (1,)))
    d_hidden_low = d_hidden.astype(bf16)

    def in_half(vector):
        zero = jnp.zeros_like(vector)
        return jnp.stack([jnp.where(on_first, vector, zero), jnp.where(on_first, zero, vector)])

    normal = centred * rstd
    q_bias = jnp.sum(d_query, axis=0, dtype=f32)
    kv_bias = jnp.sum(d_keys, axis=0, dtype=f32)
    qkv_bias = jnp.concatenate([q_bias, kv_bias]).reshape(3, half)
    cot_sum = jnp.where(on_first, jnp.sum(cotangent, axis=0, dtype=f32), 0.0)
    small = jnp.concatenate(
        [
            in_half(qkv_bias).transpose(1, 0, 2).reshape(-1),
            in_half(up_bias).reshape(-1),
            cot_sum,
            jnp.sum(d_hidden * normal, axis=0),
            jnp.sum(d_hidden, axis=0),
        ]
    ).reshape(-1, 128)

    attn_two = g_two
    out_other = lax.ppermute(out_low, "pair", both_ways)
    ahead = list(path_one[2:])
    for i, b in enumerate(path_two):
        if ahead:
            attn_one = scatter_step(attn_one, ahead.pop(0))
        attn_two = scatter_step(attn_two, b)
        attn_one, attn_two = lax.optimization_barrier((attn_one, attn_two))
        if i == len(path_two) - 1:
            attn_one, attn_two, down_all = lax.optimization_barrier(
                (attn_one, attn_two, down_all)
            )
        if i == 1:
            attn_two, d_hidden_low, small = lax.optimization_barrier(
                (attn_two, d_hidden_low, small)
            )
        if i == 2:
            attn_two, out_other = lax.optimization_barrier((attn_two, out_other))

    attn_both = jnp.stack([attn_one, attn_two])
    feed_both = feed_shard[:2]
    other = lax.ppermute(jnp.where(on_first, feed_both, attn_both), "pair", both_ways)
    zero_slot = jnp.where(on_first, attn_both, other)
    one_slot = jnp.where(on_first, other, feed_both)
    near_one = jnp.stack([zero_slot[0], one_slot[0]])[None]
    near_two = jnp.stack([zero_slot[1], one_slot[1]])[None]
    crossed = after(d_hidden_low, near_one, near_two)
    crossed = lax.ppermute(crossed, "pair", both_ways)
    small = small + lax.ppermute(small, "pair", both_ways)
    for i in range(len(bits) - 1, 0, -1):
        near_one = gather_step(near_one, path_one[i])
        near_two = gather_step(near_two, path_two[i])
        small = small + lax.ppermute(small, "seq", seq_swap(1 << path_two[i]))
        near_one, near_two, small = lax.optimization_barrier((near_one, near_two, small))
        if i == 2:
            crossed, down_all = lax.optimization_barrier((crossed, down_all, near_two))[:2]
    outputs = (widened + b_second + (out_low.astype(f32) + out_other.astype(f32))).astype(bf16)
    e = (d_hidden_low.astype(f32) + crossed.astype(f32)) * ln_gain
    d_norm = rstd * (
        e
        - jnp.mean(e, axis=1, keepdims=True)
        - normal * jnp.mean(e * normal, axis=1, keepdims=True)
    )
    d_inputs = (cotangent.astype(f32) + d_norm).astype(bf16)

    my_one = in_path(seq_at, path_one)
    my_two = in_path(seq_at, path_two)
    d_w_second = down_all.reshape(half_ff, D).astype(f32)
    near_two, outputs, d_inputs, d_w_second = lax.optimization_barrier(
        (near_two, outputs, d_inputs, d_w_second)
    )
    far_two = lax.ppermute(near_two, "seq", seq_swap(1 << path_two[0]))
    small = small + lax.ppermute(small, "seq", seq_swap(1 << path_two[0]))
    far_one = lax.ppermute(near_one, "seq", seq_swap(1 << path_one[0]))
    small = small.reshape(-1)
    if share % 32 == 0:
        low_bits = count // 2 - 1
        sel = jnp.stack([branch, core, my_one & low_bits, my_two & low_bits]).astype(jnp.int32)
        d_w_first = place_slot(near_one, far_one, near_two, far_two, sel)
    else:
        order = jnp.arange(count, dtype=jnp.int32)
        full_one = jnp.take(jnp.concatenate([near_one, far_one]), order ^ my_one, axis=0)
        full_two = jnp.take(jnp.concatenate([near_two, far_two]), order ^ my_two, axis=0)
        full_one = full_one.transpose(1, 0, 2, 3).reshape(2, D, D)
        full_two = full_two.transpose(1, 0, 2, 3).reshape(2, D, D)
        unpacked = full_one[:, :, half:].reshape(2, count, 2, share, half)
        unpacked = unpacked.transpose(0, 1, 3, 2, 4).reshape(D, D)
        as_attn = jnp.concatenate(
            [
                full_one[0, :, :half], full_one[1, :, :half],
                full_two[0, :, :half], full_two[1, :, :half],
                full_two[0, :, half:], full_two[1, :, half:],
                unpacked,
            ],
            axis=1,
        )
        as_feed = jnp.concatenate([full_one[0], full_two[0], full_one[1], full_two[1]], axis=1)
        d_w_first = jnp.where(on_first, as_attn, as_feed).astype(f32)

    cot_total = small[3 * D + FF : 4 * D + FF]
    d_b_first = jnp.where(
        on_first, jnp.concatenate([small[: 3 * D], cot_total]), small[3 * D : 3 * D + FF]
    )
    return (
        outputs,
        d_inputs,
        small[4 * D + FF : 5 * D + FF],
        small[5 * D + FF :],
        d_w_first[None],
        d_b_first[None],
        d_w_second,
        cot_total,
    )


def solution(mesh):
    in_specs = (
        P("seq", None),
        P("seq", None),
        P(),
        P(),
        P(),
        P(),
        P("pair", None, None),
        P("pair", None),
        P(),
        P(),
    )
    out_specs = (
        P("seq", None),
        P("seq", None),
        P(),
        P(),
        P("pair", None, None),
        P("pair", None),
        P("pair", None),
        P(),
    )
    return jax.shard_map(body, mesh=mesh, in_specs=in_specs, out_specs=out_specs, check_vma=False)
```
